256 devices in a mesh: rep: 2 (over z_lo), lev: 4 (over z_hi), tile: 32 (over y, x, core).
Axes of the slice: x: 4, y: 4, z: 8 (z_hi: 4, z_lo: 2; z = z_hi * 2 + z_lo), core: 2. Of those that a mesh axis runs over, the one named last changes fastest.
Arguments:
- tokens: bfloat16 [2, 8, 32, 8, 8, 768], P('rep', 'lev', 'tile'), may hold values from -6 to 6
- w_qkv: bfloat16 [768, 2304], P('tile'), may hold values from -0.21875 to 0.21875
- w_proj: bfloat16 [768, 768], P('tile'), may hold values from -0.21875 to 0.21875
- seam_codes: int32 [32, 2], replicated, may hold values from 0 to 1
- upstream: bfloat16 [2, 8, 32, 8, 8, 768], P('rep', 'lev', 'tile'), may hold values from -6 to 6
Outputs:
- output: bfloat16 [2, 8, 32, 8, 8, 768], P('rep', 'lev', 'tile')
- grad_tokens: bfloat16 [2, 8, 32, 8, 8, 768], P('rep', 'lev', 'tile')
- grad_qkv: float32 [768, 2304], P('tile')
- grad_proj: float32 [768, 768], P('tile')
The draws below stay inside these ranges and needn't reach their ends.
Inputs may be any that keep to these rules, and one draw needn't show every extreme that they name: The tiles form a periodic grid of four rows of 8 tiles: tile t's eastern neighbour is (t + 1) mod 32 and its northern neighbour (t + 8) mod 32. seam_codes[t, 0] is 1 where the seam to the eastern neighbour runs reversed, seam_codes[t, 1] likewise for the northern neighbour.
All inputs are finite; a program needn't handle non-finite values.
Results may differ from the reference program's by a relative error of at most 0.019.
Values may be sent and summed in bfloat16 or wider, within the bound.
A program may use at most 64 MiB of HBM per device.

```python
import jax
import jax.numpy as jnp
from jax import lax

D = 768
HEAD_DIM = 32
WIN = 8
WIN_LEV = 2
S = 8
LEVELS = 8
TILES = 32
BATCH = 2


def plant(array, own_key, smallest, top_value):
    longest = array.shape.index(max(array.shape))
    spots = []
    for shift in (0, 1):
        where = [jax.random.randint(jax.random.fold_in(own_key, axis), (), 0, length) for axis, length in enumerate(array.shape)]
        where[longest] = (where[longest] + shift) % array.shape[longest]
        spots.append(tuple(where))
    return array.at[spots[0]].set(smallest).at[spots[1]].set(top_value)


def spiked(result, own_key, source, target, parts, factor):
    def block_of(axis_at):
        return (jnp.arange(result.shape[axis_at]) // (result.shape[axis_at] // parts)).reshape((-1,) + (1,) * (result.ndim - 1 - axis_at))

    near = jax.random.permutation(own_key, parts)[block_of(target)]
    far = (block_of(target) + parts // 2) % parts
    return jnp.where((block_of(source) == near) | (block_of(source) == far), factor * result, result)


def block_scale(key, shape, pieces, low, high):
    def one(position, shards_of):
        steps = jax.random.uniform(jax.random.fold_in(jax.random.fold_in(key, 6), position), (shards_of,), jnp.float32, low / len(pieces), high / len(pieces))
        return jnp.repeat(jnp.exp(steps), shape[position] // shards_of).reshape((-1,) + (1,) * (len(shape) - position - 1))

    gain = one(*pieces[0])
    for cut in pieces[1:]:
        gain = gain * one(*cut)
    return gain


def gaussian(stream_key, shape, width, most, shards=(), held_as=jnp.bfloat16):
    values = width * jax.random.normal(stream_key, shape, jnp.float32)
    if shards:
        values = values * block_scale(stream_key, shape, shards, -0.22, 0.18)
    return jnp.clip(values, -most, most).astype(held_as)


def heavy_noise(key, dims, deviation, bound, cuts, heavy, kind=jnp.bfloat16):
    drawn = deviation * jax.random.normal(key, dims, jnp.float32)
    if cuts:
        drawn = drawn * block_scale(key, dims, cuts, -0.22, 0.18)
    return jnp.clip(spiked(drawn, jax.random.fold_in(key, 3), *heavy), -bound, bound).astype(kind)


def setup_inputs(seed: int = 0) -> dict:
    seeds = jax.random.split(jax.random.key(seed), 6)
    return {
        "tokens": heavy_noise(seeds[0], (BATCH, LEVELS, TILES, S, S, D), 1.0, 6.0, ((0, 2), (1, 4), (2, 32)), (2, 5, 32, 2.75)),
        "w_qkv": gaussian(seeds[1], (D, 3 * D), D ** -0.5, 0.21875, ((0, 32),)),
        "w_proj": gaussian(seeds[2], (D, D), D ** -0.5, 0.21875, ((0, 32),)),
        "seam_codes": plant(jax.random.randint(seeds[3], (TILES, 2), 0, 2), jax.random.fold_in(seeds[3], 1), 0, 1).astype(jnp.int32),
        "upstream": heavy_noise(seeds[4], (BATCH, LEVELS, TILES, S, S, D), 1.0, 6.0, ((0, 2), (1, 4), (2, 32)), (2, 5, 32, 2.75)),
    }


EPSILON = 1e-05

def layer_stats(token_rows):
    values = token_rows.astype(jnp.float32)
    center = lax.optimization_barrier(jnp.mean(values, axis=1, keepdims=True))
    spread = lax.optimization_barrier(jnp.mean(jnp.square(values - center), axis=1, keepdims=True))
    inverse = lax.rsqrt(spread + EPSILON)
    return ((values - center) * inverse, inverse)

def norm_backward(upstream_rows, grad_hidden, normalized, inverse):
    centre = lax.optimization_barrier(jnp.mean(grad_hidden, axis=1, keepdims=True))
    projected = lax.optimization_barrier(jnp.mean(grad_hidden * normalized, axis=1, keepdims=True))
    total_grad = upstream_rows.astype(jnp.float32) + (grad_hidden - centre - normalized * projected) * inverse
    return total_grad.astype(jnp.bfloat16)

def roll_field(grid_field, seam_codes, north_step):
    shift_cells = WIN // 2
    east_flag = (seam_codes[:, 0] == 1)[None, None, :, None, None, None]
    north_flag = (seam_codes[:, 1] == 1)[None, None, :, None, None, None]
    east_part = jnp.roll(grid_field, -1, axis=2)[:, :, :, :, :shift_cells]
    east_part = jnp.where(east_flag, east_part[:, :, :, ::-1], east_part)
    across = jnp.concatenate([grid_field[:, :, :, :, shift_cells:], east_part], axis=4)
    north_part = jnp.roll(across, -north_step, axis=2)[:, :, :, :shift_cells]
    north_part = jnp.where(north_flag, north_part[:, :, :, :, ::-1], north_part)
    upward = jnp.concatenate([across[:, :, :, shift_cells:], north_part], axis=3)
    return jnp.roll(upward, -1, axis=1)

def unroll_field(rolled, seam_codes, north_step):
    shift_cells = WIN // 2
    extent = rolled.shape[3]
    east_flag = (seam_codes[:, 0] == 1)[None, None, :, None, None, None]
    north_flag = (seam_codes[:, 1] == 1)[None, None, :, None, None, None]
    upward = jnp.roll(rolled, 1, axis=1)
    north_part = upward[:, :, :, extent - shift_cells:]
    north_part = jnp.where(north_flag, north_part[:, :, :, :, ::-1], north_part)
    across = jnp.concatenate([jnp.roll(north_part, north_step, axis=2), upward[:, :, :, :extent - shift_cells]], axis=3)
    east_part = across[:, :, :, :, extent - shift_cells:]
    east_part = jnp.where(east_flag, east_part[:, :, :, ::-1], east_part)
    return jnp.concatenate([jnp.roll(east_part, 1, axis=2), across[:, :, :, :, :extent - shift_cells]], axis=4)

def to_windows(grid_field):
    levels = grid_field.shape[0]
    extent = grid_field.shape[1]
    channels = grid_field.shape[3]
    blocks = grid_field.reshape(levels // WIN_LEV, WIN_LEV, extent // WIN, WIN, extent // WIN, WIN, channels)
    blocks = blocks.transpose(0, 2, 4, 1, 3, 5, 6)
    return blocks.reshape(-1, WIN_LEV * WIN * WIN, channels)

def from_windows(windows, levels, extent):
    channels = windows.shape[-1]
    blocks = windows.reshape(levels // WIN_LEV, extent // WIN, extent // WIN, WIN_LEV, WIN, WIN, channels)
    blocks = blocks.transpose(0, 3, 1, 4, 2, 5, 6)
    return blocks.reshape(levels, extent, extent, channels)

def split_heads(packed):
    windows = packed.shape[0]
    tokens = packed.shape[1]
    model_width = packed.shape[2] // 3
    head_count = model_width // HEAD_DIM
    query_part = packed[:, :, :model_width].reshape(windows, tokens, head_count, HEAD_DIM)
    key_part = packed[:, :, model_width:2 * model_width].reshape(windows, tokens, head_count, HEAD_DIM)
    value_part = packed[:, :, 2 * model_width:].reshape(windows, tokens, head_count, HEAD_DIM)
    return (query_part, key_part, value_part)

def window_mask(wrap_flags, tokens):
    level_of = jnp.arange(tokens, dtype=jnp.int32) // (WIN * WIN)
    same_level = level_of[:, None] == level_of[None, :]
    allowed = jnp.logical_or(same_level[None, None], jnp.logical_not(wrap_flags)[:, None, None, None])
    return allowed.astype(jnp.float32)

def attend_forward(packed, wrap_flags):
    query_part, key_part, value_part = split_heads(packed)
    scores = jnp.einsum('wqhd,wkhd->whqk', query_part.astype(jnp.float32), key_part.astype(jnp.float32)) * HEAD_DIM ** (-0.5)
    raised = jnp.exp(scores) * window_mask(wrap_flags, packed.shape[1])
    prob = raised / lax.optimization_barrier(jnp.sum(raised, axis=-1, keepdims=True))
    prob_low = prob.astype(jnp.bfloat16)
    attended = jnp.einsum('whqk,wkhd->wqhd', prob_low.astype(jnp.float32), value_part.astype(jnp.float32))
    attended = attended.astype(jnp.bfloat16).reshape(packed.shape[0], packed.shape[1], -1)
    return (attended, prob, prob_low)

def attend_backward(packed, back_windows, prob, prob_low):
    query_part, key_part, value_part = split_heads(packed)
    back_heads = back_windows.reshape(query_part.shape).astype(jnp.float32)
    grad_value = jnp.einsum('whqk,wqhd->wkhd', prob_low.astype(jnp.float32), back_heads)
    grad_prob = jnp.einsum('wqhd,wkhd->whqk', back_heads, value_part.astype(jnp.float32))
    centre = lax.optimization_barrier(jnp.sum(prob * grad_prob, axis=-1, keepdims=True))
    grad_scores = (prob * (grad_prob - centre) * HEAD_DIM ** (-0.5)).astype(jnp.bfloat16)
    grad_query = jnp.einsum('whqk,wkhd->wqhd', grad_scores.astype(jnp.float32), key_part.astype(jnp.float32))
    grad_key = jnp.einsum('whqk,wqhd->wkhd', grad_scores.astype(jnp.float32), query_part.astype(jnp.float32))
    windows = packed.shape[0]
    tokens = packed.shape[1]
    joined = jnp.concatenate([grad_query.reshape(windows, tokens, -1), grad_key.reshape(windows, tokens, -1), grad_value.reshape(windows, tokens, -1)], axis=-1)
    return joined.astype(jnp.bfloat16)

def reference(tokens, w_qkv, w_proj, seam_codes, upstream):
    north_step = TILES // 4
    rolled_in = roll_field(tokens, seam_codes, north_step)
    rolled_up = roll_field(upstream, seam_codes, north_step)
    lev_windows = LEVELS // WIN_LEV

    def to_blocks(grid_field):
        shaped = grid_field.reshape(BATCH, lev_windows, WIN_LEV, TILES, S, S, D)
        return shaped.transpose(0, 1, 3, 2, 4, 5, 6).reshape(-1, WIN_LEV, S, S, D)

    def from_blocks(stacked):
        shaped = stacked.reshape(BATCH, lev_windows, TILES, WIN_LEV, S, S, D)
        return shaped.transpose(0, 1, 3, 2, 4, 5, 6).reshape(BATCH, LEVELS, TILES, S, S, D)
    blocks_in = to_blocks(rolled_in)
    blocks_up = to_blocks(rolled_up)
    block_count = blocks_in.shape[0]
    wrap_all = jnp.arange(block_count, dtype=jnp.int32) // TILES % lev_windows == lev_windows - 1
    contract_last = (((1,), (1,)), ((), ()))
    contract_first = (((0,), (0,)), ((), ()))

    def block_step(running, inputs):
        tokens_block, upstream_block, wrapped = inputs
        token_rows = tokens_block.reshape(-1, D)
        upstream_rows = upstream_block.reshape(-1, D)
        normalized, inverse = layer_stats(token_rows)
        hidden = normalized.astype(jnp.bfloat16)
        projected = jnp.dot(hidden, w_qkv, preferred_element_type=jnp.float32).astype(jnp.bfloat16)
        windows_qkv = to_windows(projected.reshape(WIN_LEV, S, S, 3 * D))
        wrap_flags = jnp.full((windows_qkv.shape[0],), wrapped)
        attended, prob, prob_low = attend_forward(windows_qkv, wrap_flags)
        mixed_in = from_windows(attended, WIN_LEV, S).reshape(-1, D)
        mixed_out = lax.dot_general(mixed_in, w_proj, contract_last, preferred_element_type=jnp.float32)
        output_rows = (token_rows.astype(jnp.float32) + mixed_out).astype(jnp.bfloat16)
        back_mix = jnp.dot(upstream_rows, w_proj, preferred_element_type=jnp.float32).astype(jnp.bfloat16)
        grad_windows = attend_backward(windows_qkv, to_windows(back_mix.reshape(WIN_LEV, S, S, D)), prob, prob_low)
        grad_qkv_tok = from_windows(grad_windows, WIN_LEV, S).reshape(-1, 3 * D)
        grad_hidden = lax.dot_general(grad_qkv_tok, w_qkv, contract_last, preferred_element_type=jnp.float32)
        grad_rows = norm_backward(upstream_rows, grad_hidden, normalized, inverse)
        sum_qkv = running[0] + lax.dot_general(hidden, grad_qkv_tok, contract_first, preferred_element_type=jnp.float32)
        sum_proj = running[1] + lax.dot_general(upstream_rows, mixed_in, contract_first, preferred_element_type=jnp.float32)
        return ((sum_qkv, sum_proj), (output_rows, grad_rows))
    start_sums = (jnp.zeros((D, 3 * D), jnp.float32), jnp.zeros((D, D), jnp.float32))
    sums, stacked = lax.scan(block_step, start_sums, (blocks_in, blocks_up, wrap_all))
    output = unroll_field(from_blocks(stacked[0]), seam_codes, north_step)
    grad_tokens = unroll_field(from_blocks(stacked[1]), seam_codes, north_step)
    return (output, grad_tokens, sums[0], sums[1])
```

```python
import functools

import jax
import jax.numpy as jnp
from jax import lax
from jax.experimental import pallas as pl
from jax.experimental.pallas import tpu as pltpu
from jax.sharding import PartitionSpec as P

EPSILON = 1e-05
SCALE = 32 ** (-0.5)
MESH = pl.DeviceIdType.MESH
F32 = jnp.float32
BF16 = jnp.bfloat16
D = 768
HALF = 384
COLS = 4 * HALF
CHUNK = 48
TOK = 128

BACK = (0, 8, 1, 9)


def dot(a, b):
    return jnp.dot(a, b, preferred_element_type=F32)


def dot_t(a, b):
    return lax.dot_general(a, b, (((1,), (1,)), ((), ())), preferred_element_type=F32)


def t_dot(a, b):
    return lax.dot_general(a, b, (((0,), (0,)), ((), ())), preferred_element_type=F32)


def block_source(block_row, flag):
    group = (block_row >> 4) & 3
    n = block_row & 15
    east = group >> 1
    high = 1 - ((group & 1) ^ (flag * east))
    row = (n >> 2) + 4 * high
    col = (n & 3) + 4 * (1 - east)
    return ((block_row >> 6) << 6) + row * 8 + col


def body(
    tok_ref, upi_ref, wq_ref, wp_ref, codes_ref,
    out_ref, gt_ref, gqo_ref, gpo_ref,
    blocks, win, stage, wsib, wbuf, hid, ups, norm, inv_ref, qkv, back, mixed, gtok, opart,
    xs, xr, rsend, rrecv, grad, h2, f2, h1, f1, zs, zr, zo, za,
    roll_s, roll_r, w_s, w_r, ga_s, ga_r, gb_s, gb_r, sib_s, sib_r, par_s, par_r, ret_s, ret_r,
    h2_s, h2_r, f2_s, f2_r, h1_s, h1_r, f1_s, f1_r, z1_s, z1_r, z2_s, z2_r,
):
    rep = lax.axis_index("rep")
    lev = lax.axis_index("lev")
    tile = lax.axis_index("tile")
    core = tile % 2
    chip = tile // 2
    x = chip % 4
    y = chip // 4
    z = lev * 2 + rep
    sib_tile = chip * 2 + (1 - core)
    sib = (rep, lev, sib_tile)
    p = jnp.where(core == 0, x, y)
    q = jnp.where(core == 0, y, x)
    sp = 1 + 3 * core
    sq = 4 - 3 * core

    def chip_at(dp, dq):
        return ((p + dp + 4) % 4) * sp + ((q + dq + 4) % 4) * sq

    def at(dp, dq):
        return (rep, lev, chip_at(dp, dq) * 2 + core)

    def at_z(d, which):
        other = (z + d) % 8
        return (other % 2, other // 2, chip * 2 + which)

    def rolled(dl, dt):
        return (rep, (lev + dl + 4) % 4, (tile + dt + 32) % 32)

    def copy(src, dst, ssem, rsem, where):
        return pltpu.make_async_remote_copy(
            src_ref=src, dst_ref=dst, send_sem=ssem, recv_sem=rsem, device_id=where, device_id_type=MESH
        )

    started = []

    def send(src, dst, ssem, rsem, where):
        c = copy(src, dst, ssem, rsem, where)
        c.start()
        started.append(c)

    def arrived(dst, ssem, rsem):
        copy(dst, dst, ssem, rsem, sib).wait_recv()

    barrier = pltpu.get_barrier_semaphore()
    partners = [sib]
    partners += [(rep, lev, (y * 4 + (x + d) % 4) * 2 + core) for d in (1, 3)]
    partners += [rolled(0, dt) for dt in (1, -1, 8, -8, 9, -9)]
    partners += [rolled(-1, -dt) for dt in (1, 8, 9)] + [rolled(1, dt) for dt in (1, 8, 9)]
    partners += [at_z(d, core) for d in range(1, 8)]
    partners += [at_z(d, 1 - core) for d in range(1, 8)]
    for partner in partners:
        pl.semaphore_signal(barrier, inc=1, device_id=partner, device_id_type=MESH)

    for half in range(2):
        for kind in range(3):
            stage[half, :, kind * HALF:(kind + 1) * HALF] = wq_ref[:, kind * D + half * HALF:kind * D + (half + 1) * HALF]
        stage[half, :, 3 * HALF:] = wp_ref[:, half * HALF:(half + 1) * HALF]
    flag = codes_ref[(tile + 31) % 32, 0]
    rows_i = lax.broadcasted_iota(jnp.int32, (TOK, TOK), 0)
    cols_i = lax.broadcasted_iota(jnp.int32, (TOK, TOK), 1)
    order = (cols_i == block_source(rows_i, flag)).astype(F32).astype(BF16)
    blocks[:, :D] = dot(order, tok_ref[...]).astype(BF16)
    blocks[:, D:] = dot(order, upi_ref[...]).astype(BF16)
    pl.semaphore_wait(barrier, len(partners))

    send(stage.at[1 - core], wsib, w_s, w_r, sib)

    def span(level, group):
        return pl.ds(level * 64 + group * 16, 16)

    for level in (0, 1):
        for group in range(4):
            if level == 1 and group == 0:
                continue
            n = (1 - level) * 4 + group
            send(blocks.at[span(level, group)], win.at[span(1 - level, group)], roll_s.at[n], roll_r.at[n],
                 rolled(level - 1, -BACK[group]))
    win[0:16, :] = blocks[64:80, :]

    arrived(wsib, w_s, w_r)
    mine = stage[core].astype(F32)
    other = wsib[...].astype(F32)
    first = jnp.where(core == 0, mine, other)
    second = jnp.where(core == 0, other, mine)

    def rows_of(dp, dq):
        return pl.ds(pl.multiple_of(chip_at(dp, dq) * CHUNK, 16), CHUNK)

    wbuf[rows_of(0, 0), :] = jnp.concatenate([first, second], axis=0).astype(BF16)

    def w_at(dp, dq, half=None):
        if half is None:
            return wbuf.at[rows_of(dp, dq)]
        return wbuf.at[rows_of(dp, dq), pl.ds(half * D, D)]

    def fan_out(k, dp):
        send(w_at(dp, 0), w_at(dp, 0), gb_s.at[k, 0], gb_r.at[k, 0], at(0, 1))
        send(w_at(dp, 0), w_at(dp, 0), gb_s.at[k, 1], gb_r.at[k, 1], at(0, -1))

    def relay(k, dp):
        arrived(w_at(dp, -1), gb_s.at[k, 0], gb_r.at[k, 0])
        send(w_at(dp, -1, 0), w_at(dp, -1, 0), gb_s.at[k, 2], gb_r.at[k, 2], at(0, 1))
        arrived(w_at(dp, 1), gb_s.at[k, 1], gb_r.at[k, 1])
        send(w_at(dp, 1, 1), w_at(dp, 1, 1), gb_s.at[k, 3], gb_r.at[k, 3], at(0, -1))

    send(w_at(0, 0), w_at(0, 0), ga_s.at[0], ga_r.at[0], at(1, 0))
    send(w_at(0, 0), w_at(0, 0), ga_s.at[1], ga_r.at[1], at(-1, 0))
    fan_out(0, 0)
    arrived(w_at(-1, 0), ga_s.at[0], ga_r.at[0])
    send(w_at(-1, 0, 0), w_at(-1, 0, 0), ga_s.at[2], ga_r.at[2], at(1, 0))
    fan_out(1, -1)
    arrived(w_at(1, 0), ga_s.at[1], ga_r.at[1])
    send(w_at(1, 0, 1), w_at(1, 0, 1), ga_s.at[3], ga_r.at[3], at(-1, 0))
    fan_out(2, 1)
    relay(0, 0)
    arrived(w_at(2, 0, 0), ga_s.at[2], ga_r.at[2])
    arrived(w_at(2, 0, 1), ga_s.at[3], ga_r.at[3])
    fan_out(3, 2)
    relay(1, -1)
    relay(2, 1)

    for n in range(1, 8):
        arrived(win.at[pl.ds(n * 16, 16)], roll_s.at[n], roll_r.at[n])
    my_rows = pl.ds(pl.multiple_of(core * TOK, TOK), TOK)
    ups[my_rows, :] = win[:, D:]
    send(ups.at[my_rows], ups.at[my_rows], sib_s.at[1], sib_r.at[1], sib)
    values = win[:, :D].astype(F32)
    centred = values - jnp.mean(values, axis=1, keepdims=True)
    inverse = lax.rsqrt(jnp.mean(jnp.square(centred), axis=1, keepdims=True) + EPSILON)
    normalized = centred * inverse
    norm[...] = normalized
    inv_ref[...] = jnp.broadcast_to(inverse, (TOK, 128))
    hid[my_rows, :] = normalized.astype(BF16)
    send(hid.at[my_rows], hid.at[my_rows], sib_s.at[0], sib_r.at[0], sib)
    relay(3, 2)
    their_rows = pl.ds(pl.multiple_of((1 - core) * TOK, TOK), TOK)
    arrived(hid.at[their_rows], sib_s.at[0], sib_r.at[0])
    arrived(ups.at[their_rows], sib_s.at[1], sib_r.at[1])
    for k, dp in enumerate((0, -1, 1, 2)):
        arrived(w_at(dp, 2, 0), gb_s.at[k, 2], gb_r.at[k, 2])
        arrived(w_at(dp, 2, 1), gb_s.at[k, 3], gb_r.at[k, 3])

    qkv[...] = dot(hid[...], wbuf[:, :3 * HALF]).astype(BF16)
    back[...] = dot(ups[...], wbuf[:, 3 * HALF:]).astype(BF16)
    allow = jnp.where(lev == 3, jnp.where((rows_i >> 6) == (cols_i >> 6), 1.0, 0.0), 1.0).astype(F32)
    allow = jnp.concatenate([allow] * 4, axis=0)
    lane_head = lax.broadcasted_iota(jnp.int32, (TOK, 128), 1) >> 5
    head_masks = [(lane_head == h).astype(F32).astype(BF16) for h in range(4)]

    def stacked(part):
        return jnp.concatenate([part * m for m in head_masks], axis=0)

    def beside(part):
        return jnp.concatenate([part[h * TOK:(h + 1) * TOK] for h in range(4)], axis=1)

    for w in range(2):
        rows = slice(w * TOK, (w + 1) * TOK)
        for j in range(3):
            lanes = [slice(kind * HALF + j * 128, kind * HALF + (j + 1) * 128) for kind in range(3)]
            query, key, value = (qkv[rows, s] for s in lanes)
            coming = back[rows, lanes[0]]
            query_s, key_s, value_s, coming_s = (stacked(a) for a in (query, key, value, coming))
            raised = jnp.exp(dot_t(query_s, key) * SCALE) * allow
            prob = raised * (1.0 / jnp.sum(raised, axis=1, keepdims=True))
            low = prob.astype(BF16)
            mixed[rows, lanes[0]] = dot(beside(low), value_s).astype(BF16)
            grad_prob = dot_t(coming_s, value)
            centre = jnp.sum(prob * grad_prob, axis=1, keepdims=True)
            grad_scores = (prob * (grad_prob - centre) * SCALE).astype(BF16)
            gtok[rows, lanes[0]] = dot(beside(grad_scores), key_s).astype(BF16)
            gtok[rows, lanes[1]] = t_dot(grad_scores, query_s).astype(BF16)
            gtok[rows, lanes[2]] = t_dot(low, coming_s).astype(BF16)

    grad[:, :3 * HALF] = t_dot(hid[...], gtok[...]).astype(BF16)
    grad[:, 3 * HALF:] = t_dot(ups[...], mixed[...]).astype(BF16)

    def g_at(dp, dq, half=None):
        if half is None:
            return grad.at[rows_of(dp, dq)]
        return grad.at[rows_of(dp, dq), pl.ds(half * D, D)]

    along = (2, 1, -1, 0)
    for k, dp in enumerate(along):
        send(g_at(dp, 2, 0), h2.at[0, k], h2_s.at[0, k], h2_r.at[0, k], at(0, 1))
        send(g_at(dp, 2, 1), h2.at[1, k], h2_s.at[1, k], h2_r.at[1, k], at(0, -1))

    opart[:, :D] = dot_t(mixed[...], wbuf[:, 3 * HALF:])
    opart[:, D:] = dot_t(gtok[...], wbuf[:, :3 * HALF])
    xs[...] = opart[their_rows, :].astype(BF16)
    send(xs, xr, par_s, par_r, sib)

    def add_half(dp, dq, half, k):
        where = (rows_of(dp, dq), pl.ds(half * D, D))
        grad[where] = (grad[where].astype(F32) + h2[half, k].astype(F32)).astype(BF16)

    for k, dp in enumerate(along):
        arrived(h2.at[0, k], h2_s.at[0, k], h2_r.at[0, k])
        add_half(dp, 1, 0, k)
        send(g_at(dp, 1), f2.at[0, k], f2_s.at[0, k], f2_r.at[0, k], at(0, 1))
        arrived(h2.at[1, k], h2_s.at[1, k], h2_r.at[1, k])
        add_half(dp, -1, 1, k)
        send(g_at(dp, -1), f2.at[1, k], f2_s.at[1, k], f2_r.at[1, k], at(0, -1))

    arrived(xr, par_s, par_r)
    total = win[:, :D].astype(F32) + opart[my_rows, :D] + xr[:, :D].astype(F32)
    rsend[:, :D] = total.astype(BF16)
    grad_hidden = opart[my_rows, D:] + xr[:, D:].astype(F32)
    normalized = norm[...]
    centre = jnp.mean(grad_hidden, axis=1, keepdims=True)
    along_norm = jnp.mean(grad_hidden * normalized, axis=1, keepdims=True)
    moved = (grad_hidden - centre - normalized * along_norm) * inv_ref[:, :1]
    rsend[:, D:] = (win[:, D:].astype(F32) + moved).astype(BF16)
    for level in (0, 1):
        for group in range(4):
            if level == 1 and group == 0:
                continue
            n = level * 4 + group if level == 0 else 4 + group
            send(rsend.at[span(1 - level, group)], rrecv.at[span(level, group)], ret_s.at[n], ret_r.at[n],
                 rolled(1 - level, BACK[group]))
    rrecv[64:80, :] = rsend[0:16, :]

    def sum_second(k, dp):
        arrived(f2.at[0, k], f2_s.at[0, k], f2_r.at[0, k])
        arrived(f2.at[1, k], f2_s.at[1, k], f2_r.at[1, k])
        return grad[rows_of(dp, 0), :].astype(F32) + f2[0, k].astype(F32) + f2[1, k].astype(F32)

    grad[rows_of(2, 0), :] = sum_second(0, 2).astype(BF16)
    send(g_at(2, 0, 0), h1.at[0], h1_s.at[0], h1_r.at[0], at(1, 0))
    send(g_at(2, 0, 1), h1.at[1], h1_s.at[1], h1_r.at[1], at(-1, 0))
    for side, dp in ((0, 1), (1, -1)):
        partial = sum_second(1 + side, dp)
        arrived(h1.at[side], h1_s.at[side], h1_r.at[side])
        grad[rows_of(dp, 0), :] = partial.astype(BF16)
        where = (rows_of(dp, 0), pl.ds(side * D, D))
        grad[where] = (partial[:, side * D:(side + 1) * D] + h1[side].astype(F32)).astype(BF16)
        send(g_at(dp, 0), f1.at[side], f1_s.at[side], f1_r.at[side], at(dp, 0))
    plane = sum_second(3, 0)
    for side in range(2):
        arrived(f1.at[side], f1_s.at[side], f1_r.at[side])
        plane = plane + f1[side].astype(F32)

    for piece in range(8):
        kind, r = piece // 2, piece % 2
        zs[piece] = plane[r * 24:(r + 1) * 24, kind * HALF:(kind + 1) * HALF].astype(BF16)
    for d in range(1, 8):
        send(zs.at[(z + d) % 8], zr.at[d], z1_s.at[d], z1_r.at[d], at_z(d, core))

    for n in range(8):
        if n != 4:
            arrived(rrecv.at[pl.ds(n * 16, 16)], ret_s.at[n], ret_r.at[n])
    order_t = (rows_i == block_source(cols_i, flag)).astype(F32).astype(BF16)
    out_ref[...] = dot(order_t, rrecv[:, :D]).astype(BF16)
    gt_ref[...] = dot(order_t, rrecv[:, D:]).astype(BF16)

    total = zs[z].astype(F32)
    for d in range(1, 8):
        arrived(zr.at[d], z1_s.at[d], z1_r.at[d])
        total = total + zr[d].astype(F32)
    zo[...] = total.astype(BF16)
    r = z % 2
    slot = (z // 2) * 2 + core
    last = [copy(zo, za.at[slot], z2_s.at[d], z2_r.at[slot], at_z(d, r)) for d in range(8)]
    for d in range(1, 8):
        last[d].start()

    @pl.when(r == core)
    def _():
        za[slot] = zo[...]

    @pl.when(r != core)
    def _():
        last[0].start()

    for n in range(8):
        own = jnp.logical_and(r == core, slot == n)

        @pl.when(jnp.logical_not(own))
        def _():
            arrived(za.at[n], z2_s.at[0], z2_r.at[n])

    for kind in range(4):
        for half in range(2):
            piece = za[kind * 2 + half].astype(F32)
            if kind < 3:
                gqo_ref[:, kind * D + half * HALF:kind * D + (half + 1) * HALF] = piece
            else:
                gpo_ref[:, half * HALF:(half + 1) * HALF] = piece

    for c in started + last[1:]:
        c.wait_send()

    @pl.when(r != core)
    def _():
        last[0].wait_send()


def shards(tokens, w_qkv, w_proj, seam_codes, upstream):
    dma = pltpu.SemaphoreType.DMA
    vmem = pltpu.VMEM
    scratch = [
        vmem((TOK, 2 * D), BF16),
        vmem((TOK, 2 * D), BF16),
        vmem((2, 24, COLS), BF16),
        vmem((24, COLS), BF16),
        vmem((D, COLS), BF16),
        vmem((2 * TOK, D), BF16),
        vmem((2 * TOK, D), BF16),
        vmem((TOK, D), F32),
        vmem((TOK, 128), F32),
        vmem((2 * TOK, 3 * HALF), BF16),
        vmem((2 * TOK, HALF), BF16),
        vmem((2 * TOK, HALF), BF16),
        vmem((2 * TOK, 3 * HALF), BF16),
        vmem((2 * TOK, 2 * D), F32),
        vmem((TOK, 2 * D), BF16),
        vmem((TOK, 2 * D), BF16),
        vmem((TOK, 2 * D), BF16),
        vmem((TOK, 2 * D), BF16),
        vmem((D, COLS), BF16),
        vmem((2, 4, CHUNK, D), BF16),
        vmem((2, 4, CHUNK, COLS), BF16),
        vmem((2, CHUNK, D), BF16),
        vmem((2, CHUNK, COLS), BF16),
        vmem((8, 24, HALF), BF16),
        vmem((8, 24, HALF), BF16),
        vmem((24, HALF), BF16),
        vmem((8, 24, HALF), BF16),
        dma((8,)), dma((8,)),
        dma, dma,
        dma((4,)), dma((4,)),
        dma((4, 4)), dma((4, 4)),
        dma((2,)), dma((2,)),
        dma, dma,
        dma((8,)), dma((8,)),
        dma((2, 4)), dma((2, 4)), dma((2, 4)), dma((2, 4)),
        dma((2,)), dma((2,)), dma((2,)), dma((2,)),
        dma((8,)), dma((8,)), dma((8,)), dma((8,)),
    ]
    in_vmem = pl.BlockSpec(memory_space=pltpu.VMEM)
    out, grad_tok, grad_qkv, grad_proj = pl.pallas_call(
        body,
        out_shape=(
            jax.ShapeDtypeStruct((TOK, D), BF16),
            jax.ShapeDtypeStruct((TOK, D), BF16),
            jax.ShapeDtypeStruct((24, 3 * D), F32),
            jax.ShapeDtypeStruct((24, D), F32),
        ),
        in_specs=[in_vmem] * 4 + [pl.BlockSpec(memory_space=pltpu.SMEM)],
        out_specs=(in_vmem,) * 4,
        scratch_shapes=scratch,
        compiler_params=pltpu.CompilerParams(
            collective_id=0, has_side_effects=True, vmem_limit_bytes=48 * 1024 * 1024
        ),
        name="layer",
    )(tokens.reshape(TOK, D), upstream.reshape(TOK, D), w_qkv, w_proj, seam_codes)
    return (out.reshape(tokens.shape), grad_tok.reshape(tokens.shape), grad_qkv, grad_proj)


def solution(mesh):
    field = P("rep", "lev", "tile", None, None, None)
    rows = P("tile", None)
    return jax.shard_map(
        shards,
        mesh=mesh,
        in_specs=(field, rows, rows, P(), field),
        out_specs=(field, field, rows, rows),
        check_vma=False,
    )
```

```python
import functools

import jax
import jax.numpy as jnp
from jax import lax
from jax.experimental import pallas as pl
from jax.experimental.pallas import tpu as pltpu
from jax.sharding import PartitionSpec as P

EPSILON = 1e-05
SCALE = 32 ** (-0.5)
MESH = pl.DeviceIdType.MESH
F32 = jnp.float32
BF16 = jnp.bfloat16
D = 768
HALF = 384
COLS = 4 * HALF
GROUPS = 3
WIDE = COLS // GROUPS
CHUNK = 48
TOK = 128

BACK = (0, 8, 1, 9)


def dot(a, b):
    return jnp.dot(a, b, preferred_element_type=F32)


def dot_t(a, b):
    return lax.dot_general(a, b, (((1,), (1,)), ((), ())), preferred_element_type=F32)


def t_dot(a, b):
    return lax.dot_general(a, b, (((0,), (0,)), ((), ())), preferred_element_type=F32)


def block_source(block_row, flag):
    group = (block_row >> 4) & 3
    n = block_row & 15
    east = group >> 1
    high = 1 - ((group & 1) ^ (flag * east))
    row = (n >> 2) + 4 * high
    col = (n & 3) + 4 * (1 - east)
    return ((block_row >> 6) << 6) + row * 8 + col


def body(
    tok_hbm, upi_hbm, wq_hbm, wp_hbm, codes_hbm,
    out_hbm, gt_hbm, gqo_hbm, gpo_hbm,
    tok, upi, wq, wp, codes, blocks, win, stage, wsib, wbuf, wnat, hid, ups, hid_t, ups_t, norm, inv_ref,
    qkv, back, mixed, gtok, opart, xs, xr, rsend, rrecv, grad, h2, f2, psum, f1, zs, zr, zo, za,
    out_v, gt_v, gqo_v, gpo_v,
    in_sem, out_sem,
    roll_s, roll_r, w_s, w_r, ga_s, ga_r, gb_s, gb_r, sib_s, sib_r, par_s, par_r, ret_s, ret_r,
    h2_s, h2_r, f2_s, f2_r, f1_s, f1_r, z1_s, z1_r, z2_s, z2_r,
):
    fetched = [
        pltpu.make_async_copy(a, b, in_sem.at[i])
        for i, (a, b) in enumerate(((wq_hbm, wq), (wp_hbm, wp), (codes_hbm, codes), (tok_hbm, tok), (upi_hbm, upi)))
    ]
    for c in fetched:
        c.start()

    rep = lax.axis_index("rep")
    lev = lax.axis_index("lev")
    tile = lax.axis_index("tile")
    core = tile % 2
    chip = tile // 2
    x = chip % 4
    y = chip // 4
    z = lev * 2 + rep
    sib = (rep, lev, chip * 2 + (1 - core))
    p = jnp.where(core == 0, x, y)
    q = jnp.where(core == 0, y, x)
    sp = 1 + 3 * core
    sq = 4 - 3 * core

    def around(value, step):
        return (value + step + 4) % 4

    def at(dp, dq):
        return (rep, lev, (around(p, dp) * sp + around(q, dq) * sq) * 2 + core)

    def at_z(d, where):
        other = (z + d + 8) % 8
        return (other % 2, other // 2, where)

    def near(dz, dt):
        return at_z(dz, (tile + dt + 32) % 32)

    def copy(src, dst, ssem, rsem, where):
        return pltpu.make_async_remote_copy(
            src_ref=src, dst_ref=dst, send_sem=ssem, recv_sem=rsem, device_id=where, device_id_type=MESH
        )

    started = []

    def send(src, dst, ssem, rsem, where):
        c = copy(src, dst, ssem, rsem, where)
        c.start()
        started.append(c)

    def arrived(dst, ssem, rsem):
        copy(dst, dst, ssem, rsem, sib).wait_recv()

    barrier = pltpu.get_barrier_semaphore()
    partners = [sib]
    partners += [at(d, 0) for d in (1, 2, 3)] + [at(0, d) for d in (1, 2, 3)]
    partners += [near(dz, dt) for dz in (1, -1) for dt in (1, -1, 8, -8, 9, -9)]
    partners += [at_z(d, chip * 2 + c) for d in range(1, 8) for c in (0, 1)]
    for partner in partners:
        pl.semaphore_signal(barrier, inc=1, device_id=partner, device_id_type=MESH)

    fetched[0].wait()
    fetched[1].wait()
    for half in range(2):
        for j in range(GROUPS):
            for kind in range(3):
                at_col = kind * D + half * HALF + j * 128
                stage[half, :, j * WIDE + kind * 128:j * WIDE + (kind + 1) * 128] = wq[:, at_col:at_col + 128]
            at_col = half * HALF + j * 128
            stage[half, :, j * WIDE + 384:(j + 1) * WIDE] = wp[:, at_col:at_col + 128]
    for c in fetched[2:]:
        c.wait()
    flag = codes[0, (tile + 31) % 32]
    rows_i = lax.broadcasted_iota(jnp.int32, (TOK, TOK), 0)
    cols_i = lax.broadcasted_iota(jnp.int32, (TOK, TOK), 1)
    order = (cols_i == block_source(rows_i, flag)).astype(F32).astype(BF16)
    blocks[:, :D] = dot(order, tok[...]).astype(BF16)
    blocks[:, D:] = dot(order, upi[...]).astype(BF16)
    pl.semaphore_wait(barrier, len(partners))

    send(stage.at[1 - core], wsib, w_s, w_r, sib)

    def span(level, group):
        return pl.ds(level * 64 + group * 16, 16)

    for group in range(4):
        for level, dz in ((1, 1), (0, -1)):
            n = (1 - level) * 4 + group
            send(blocks.at[span(level, group)], win.at[span(1 - level, group)], roll_s.at[n], roll_r.at[n],
                 near(dz, -BACK[group]))

    arrived(wsib, w_s, w_r)
    mine = stage[core].astype(F32)
    other = wsib[...].astype(F32)
    first = jnp.where(core == 0, mine, other)
    second = jnp.where(core == 0, other, mine)
    chunk = jnp.concatenate([first, second], axis=0).astype(BF16)
    for j in range(GROUPS):
        wbuf[j, q * 4 + p] = chunk[:, j * WIDE:(j + 1) * WIDE]

    def line(buf, j, dq, start=0, count=4):
        return buf.at[j, pl.ds(around(q, dq) * 4 + start, count)]

    def gather_first(j):
        own = wbuf.at[j, q * 4 + p]
        for d in (1, 3, 2):
            send(own, own, ga_s.at[j, d], ga_r.at[j, d], at(d, 0))

    def gather_second(j):
        for d in (1, 2, 3):
            arrived(wbuf.at[j, q * 4 + around(p, -d)], ga_s.at[j, d], ga_r.at[j, d])
        send(line(wbuf, j, 0), line(wbuf, j, 0), gb_s.at[j, 0], gb_r.at[j, 0], at(0, 1))
        send(line(wbuf, j, 0), line(wbuf, j, 0), gb_s.at[j, 1], gb_r.at[j, 1], at(0, -1))

    def gather_relay(j):
        arrived(line(wbuf, j, -1), gb_s.at[j, 0], gb_r.at[j, 0])
        send(line(wbuf, j, -1, 0, 2), line(wbuf, j, -1, 0, 2), gb_s.at[j, 2], gb_r.at[j, 2], at(0, 1))
        arrived(line(wbuf, j, 1), gb_s.at[j, 1], gb_r.at[j, 1])
        send(line(wbuf, j, 1, 2, 2), line(wbuf, j, 1, 2, 2), gb_s.at[j, 3], gb_r.at[j, 3], at(0, -1))

    def natural(n):
        return n + core * ((n % 4) * 4 + n // 4 - n)

    def gather_end(j):
        arrived(line(wbuf, j, 2, 0, 2), gb_s.at[j, 2], gb_r.at[j, 2])
        arrived(line(wbuf, j, 2, 2, 2), gb_s.at[j, 3], gb_r.at[j, 3])
        for n in range(16):
            wnat[j, n * CHUNK:(n + 1) * CHUNK, :] = wbuf[j, natural(n)]

    for j in range(GROUPS):
        gather_first(j)
    for j in range(GROUPS):
        gather_second(j)
    gather_relay(0)

    for n in range(8):
        arrived(win.at[pl.ds(n * 16, 16)], roll_s.at[n], roll_r.at[n])
    my_rows = pl.ds(pl.multiple_of(core * TOK, TOK), TOK)
    their_rows = pl.ds(pl.multiple_of((1 - core) * TOK, TOK), TOK)
    ups[my_rows, :] = win[:, D:]
    send(ups.at[my_rows], ups.at[my_rows], sib_s.at[1], sib_r.at[1], sib)
    values = win[:, :D].astype(F32)
    centred = values - jnp.mean(values, axis=1, keepdims=True)
    inverse = lax.rsqrt(jnp.mean(jnp.square(centred), axis=1, keepdims=True) + EPSILON)
    normalized = centred * inverse
    norm[...] = normalized
    inv_ref[...] = jnp.broadcast_to(inverse, (TOK, 128))
    hid[my_rows, :] = normalized.astype(BF16)
    send(hid.at[my_rows], hid.at[my_rows], sib_s.at[0], sib_r.at[0], sib)
    gather_relay(1)
    arrived(ups.at[their_rows], sib_s.at[1], sib_r.at[1])
    arrived(hid.at[their_rows], sib_s.at[0], sib_r.at[0])
    hid_t[...] = hid[...].T
    ups_t[...] = ups[...].T

    wrapped = jnp.logical_or(z == 0, z == 7)
    allow = jnp.where(wrapped, jnp.where((rows_i >> 6) == (cols_i >> 6), 1.0, 0.0), 1.0).astype(F32)
    allow = jnp.concatenate([allow] * 4, axis=0)
    lane_head = lax.broadcasted_iota(jnp.int32, (TOK, 128), 1) >> 5
    head_masks = [(lane_head == h).astype(F32).astype(BF16) for h in range(4)]

    def stacked(part):
        return jnp.concatenate([part * m for m in head_masks], axis=0)

    def beside(part):
        return jnp.concatenate([part[h * TOK:(h + 1) * TOK] for h in range(4)], axis=1)

    def attention(j):
        qkv[...] = dot(hid[...], wnat[j, :, :384]).astype(BF16)
        back[...] = dot(ups[...], wnat[j, :, 384:]).astype(BF16)
        for w in range(2):
            rows = slice(w * TOK, (w + 1) * TOK)
            query, key, value = (qkv[rows, kind * 128:(kind + 1) * 128] for kind in range(3))
            coming = back[rows, :]
            query_s, key_s, value_s, coming_s = (stacked(a) for a in (query, key, value, coming))
            raised = jnp.exp(dot_t(query_s, key) * SCALE) * allow
            prob = raised * (1.0 / jnp.sum(raised, axis=1, keepdims=True))
            low = prob.astype(BF16)
            mixed[j, rows, :] = dot(beside(low), value_s).astype(BF16)
            grad_prob = dot_t(coming_s, value)
            centre = jnp.sum(prob * grad_prob, axis=1, keepdims=True)
            grad_scores = (prob * (grad_prob - centre) * SCALE).astype(BF16)
            gtok[j, rows, 0:128] = dot(beside(grad_scores), key_s).astype(BF16)
            gtok[j, rows, 128:256] = t_dot(grad_scores, query_s).astype(BF16)
            gtok[j, rows, 256:384] = t_dot(low, coming_s).astype(BF16)
        grad_q = dot(hid_t[...], gtok[j]).astype(BF16)
        grad_p = dot(ups_t[...], mixed[j]).astype(BF16)
        for n in range(16):
            part = slice(n * CHUNK, (n + 1) * CHUNK)
            grad[j, natural(n), :, :384] = grad_q[part]
            grad[j, natural(n), :, 384:] = grad_p[part]

    def outputs_share(j):
        to_output = dot_t(mixed[j], wnat[j, :, 384:])
        to_hidden = dot_t(gtok[j], wnat[j, :, :384])
        if j == 0:
            opart[:, :D] = to_output
            opart[:, D:] = to_hidden
        else:
            opart[:, :D] += to_output
            opart[:, D:] += to_hidden

    def sum_start(j):
        send(line(grad, j, 2, 0, 2), h2.at[j, 0], h2_s.at[j, 0], h2_r.at[j, 0], at(0, 1))
        send(line(grad, j, 2, 2, 2), h2.at[j, 1], h2_s.at[j, 1], h2_r.at[j, 1], at(0, -1))

    def sum_relay(j):
        for side, dq in ((0, 1), (1, -1)):
            arrived(h2.at[j, side], h2_s.at[j, side], h2_r.at[j, side])
            for k in range(2):
                place = around(q, dq) * 4 + 2 * side + k
                grad[j, place] = (grad[j, place].astype(F32) + h2[j, side, k].astype(F32)).astype(BF16)
            send(line(grad, j, dq), f2.at[j, side], f2_s.at[j, side], f2_r.at[j, side], at(0, dq))

    def sum_first(j):
        for side in range(2):
            arrived(f2.at[j, side], f2_s.at[j, side], f2_r.at[j, side])
        for k in range(4):
            total = grad[j, q * 4 + k].astype(F32) + f2[j, 0, k].astype(F32) + f2[j, 1, k].astype(F32)
            psum[j, k] = total.astype(BF16)
        for d in (2, 1, 3):
            send(psum.at[j, around(p, d)], f1.at[j, d], f1_s.at[j, d], f1_r.at[j, d], at(d, 0))

    def sum_z(j):
        total = psum[j, p].astype(F32)
        for d in (1, 3, 2):
            arrived(f1.at[j, d], f1_s.at[j, d], f1_r.at[j, d])
            total = total + f1[j, d].astype(F32)
        for kind in range(4):
            for r in range(2):
                zs[j, kind * 2 + r] = total[r * 24:(r + 1) * 24, kind * 128:(kind + 1) * 128].astype(BF16)
        for d in (4, 3, 5, 2, 6, 1, 7):
            send(zs.at[j, (z + d) % 8], zr.at[j, d], z1_s.at[j, d], z1_r.at[j, d], at_z(d, chip * 2 + core))

    half_here = z % 2
    slot = (z // 2) * 2 + core
    to_sibling = []

    def hand_out(j):
        total = zs[j, z].astype(F32)
        for d in range(1, 8):
            arrived(zr.at[j, d], z1_s.at[j, d], z1_r.at[j, d])
            total = total + zr[j, d].astype(F32)
        zo[j] = total.astype(BF16)
        for d in (4, 3, 5, 2, 6, 1, 7):
            send(zo.at[j], za.at[j, slot], z2_s.at[j, d], z2_r.at[j, slot], at_z(d, chip * 2 + half_here))
        here = copy(zo.at[j], za.at[j, slot], z2_s.at[j, 0], z2_r.at[j, slot], sib)
        to_sibling.append(here)

        @pl.when(half_here == core)
        def _():
            za[j, slot] = zo[j]

        @pl.when(half_here != core)
        def _():
            here.start()

    def finish(j):
        for n in range(8):
            own = jnp.logical_and(half_here == core, slot == n)

            @pl.when(jnp.logical_not(own))
            def _():
                arrived(za.at[j, n], z2_s.at[j, 0], z2_r.at[j, n])
        for kind in range(4):
            for half in range(2):
                piece = za[j, kind * 2 + half].astype(F32)
                at_col = half * HALF + j * 128
                if kind < 3:
                    gqo_v[:, kind * D + at_col:kind * D + at_col + 128] = piece
                else:
                    gpo_v[:, at_col:at_col + 128] = piece

    gather_end(0)
    attention(0)
    sum_start(0)
    gather_relay(2)
    outputs_share(0)
    gather_end(1)
    attention(1)
    sum_start(1)
    sum_relay(0)
    outputs_share(1)
    gather_end(2)
    attention(2)
    sum_start(2)
    outputs_share(2)
    xs[...] = opart[their_rows, :].astype(BF16)
    send(xs, xr, par_s, par_r, sib)
    sum_relay(1)
    sum_first(0)

    arrived(xr, par_s, par_r)
    total = win[:, :D].astype(F32) + opart[my_rows, :D] + xr[:, :D].astype(F32)
    rsend[:, :D] = total.astype(BF16)
    grad_hidden = opart[my_rows, D:] + xr[:, D:].astype(F32)
    normalized = norm[...]
    centre = jnp.mean(grad_hidden, axis=1, keepdims=True)
    along_norm = jnp.mean(grad_hidden * normalized, axis=1, keepdims=True)
    moved = (grad_hidden - centre - normalized * along_norm) * inv_ref[:, :1]
    rsend[:, D:] = (win[:, D:].astype(F32) + moved).astype(BF16)
    for group in range(4):
        for level, dz in ((1, -1), (0, 1)):
            n = level * 4 + group
            send(rsend.at[span(1 - level, group)], rrecv.at[span(level, group)], ret_s.at[n], ret_r.at[n],
                 near(dz, BACK[group]))

    sum_relay(2)
    sum_first(1)
    sum_z(0)
    sum_first(2)
    sum_z(1)
    hand_out(0)
    sum_z(2)
    hand_out(1)

    for n in range(8):
        arrived(rrecv.at[pl.ds(n * 16, 16)], ret_s.at[n], ret_r.at[n])
    order_t = (rows_i == block_source(cols_i, flag)).astype(F32).astype(BF16)
    out_v[...] = dot(order_t, rrecv[:, :D]).astype(BF16)
    gt_v[...] = dot(order_t, rrecv[:, D:]).astype(BF16)
    written = [
        pltpu.make_async_copy(a, b, out_sem.at[i])
        for i, (a, b) in enumerate(((out_v, out_hbm), (gt_v, gt_hbm), (gqo_v, gqo_hbm), (gpo_v, gpo_hbm)))
    ]
    written[0].start()
    written[1].start()
    hand_out(2)
    finish(0)
    finish(1)
    finish(2)
    written[2].start()
    written[3].start()
    for c in started:
        c.wait_send()

    @pl.when(half_here != core)
    def _():
        for c in to_sibling:
            c.wait_send()

    for c in written:
        c.wait()


def place_body(*refs):
    ins, outs, held, sem = refs[:4], refs[4:8], refs[8:12], refs[12]
    reads = [pltpu.make_async_copy(a, b, sem.at[0, i]) for i, (a, b) in enumerate(zip(ins, held))]
    writes = [pltpu.make_async_copy(a, b, sem.at[1, i]) for i, (a, b) in enumerate(zip(held, outs))]
    for c in reads:
        c.start()
    for r, w in zip(reads, writes):
        r.wait()
        w.start()
    for c in writes:
        c.wait()


def shards(tokens, w_qkv, w_proj, seam_codes, upstream):
    dma = pltpu.SemaphoreType.DMA
    vmem = pltpu.VMEM
    scratch = [
        vmem((TOK, D), BF16),
        vmem((TOK, D), BF16),
        vmem((24, 3 * D), BF16),
        vmem((24, D), BF16),
        pltpu.SMEM((2, 32), jnp.int32),
        vmem((TOK, 2 * D), BF16),
        vmem((TOK, 2 * D), BF16),
        vmem((2, 24, COLS), BF16),
        vmem((24, COLS), BF16),
        vmem((GROUPS, 16, CHUNK, WIDE), BF16),
        vmem((GROUPS, D, WIDE), BF16),
        vmem((2 * TOK, D), BF16),
        vmem((2 * TOK, D), BF16),
        vmem((D, 2 * TOK), BF16),
        vmem((D, 2 * TOK), BF16),
        vmem((TOK, D), F32),
        vmem((TOK, 128), F32),
        vmem((2 * TOK, 384), BF16),
        vmem((2 * TOK, 128), BF16),
        vmem((GROUPS, 2 * TOK, 128), BF16),
        vmem((GROUPS, 2 * TOK, 384), BF16),
        vmem((2 * TOK, 2 * D), F32),
        vmem((TOK, 2 * D), BF16),
        vmem((TOK, 2 * D), BF16),
        vmem((TOK, 2 * D), BF16),
        vmem((TOK, 2 * D), BF16),
        vmem((GROUPS, 16, CHUNK, WIDE), BF16),
        vmem((GROUPS, 2, 2, CHUNK, WIDE), BF16),
        vmem((GROUPS, 2, 4, CHUNK, WIDE), BF16),
        vmem((GROUPS, 4, CHUNK, WIDE), BF16),
        vmem((GROUPS, 4, CHUNK, WIDE), BF16),
        vmem((GROUPS, 8, 24, 128), BF16),
        vmem((GROUPS, 8, 24, 128), BF16),
        vmem((GROUPS, 24, 128), BF16),
        vmem((GROUPS, 8, 24, 128), BF16),
        vmem((TOK, D), BF16),
        vmem((TOK, D), BF16),
        vmem((24, 3 * D), F32),
        vmem((24, D), F32),
        dma((5,)), dma((4,)),
        dma((8,)), dma((8,)),
        dma, dma,
        dma((GROUPS, 4)), dma((GROUPS, 4)),
        dma((GROUPS, 4)), dma((GROUPS, 4)),
        dma((2,)), dma((2,)),
        dma, dma,
        dma((8,)), dma((8,)),
        dma((GROUPS, 2)), dma((GROUPS, 2)),
        dma((GROUPS, 2)), dma((GROUPS, 2)),
        dma((GROUPS, 4)), dma((GROUPS, 4)),
        dma((GROUPS, 8)), dma((GROUPS, 8)), dma((GROUPS, 8)), dma((GROUPS, 8)),
    ]
    anywhere = pl.BlockSpec(memory_space=pl.ANY)
    shapes = (
        jax.ShapeDtypeStruct((TOK, D), BF16),
        jax.ShapeDtypeStruct((TOK, D), BF16),
        jax.ShapeDtypeStruct((24, 3 * D), F32),
        jax.ShapeDtypeStruct((24, D), F32),
    )
    results = pl.pallas_call(
        body,
        out_shape=shapes,
        in_specs=[anywhere] * 5,
        out_specs=(anywhere,) * 4,
        scratch_shapes=scratch,
        compiler_params=pltpu.CompilerParams(
            collective_id=0, has_side_effects=True, vmem_limit_bytes=56 * 1024 * 1024
        ),
        name="layer",
    )(tokens.reshape(TOK, D), upstream.reshape(TOK, D), w_qkv, w_proj, seam_codes.T)
    out, grad_tok, grad_qkv, grad_proj = pl.pallas_call(
        place_body,
        out_shape=shapes,
        in_specs=[anywhere] * 4,
        out_specs=(anywhere,) * 4,
        scratch_shapes=[vmem(a.shape, a.dtype) for a in shapes] + [dma((2, 4))],
        name="place",
    )(*results)
    return (out.reshape(tokens.shape), grad_tok.reshape(tokens.shape), grad_qkv, grad_proj)


def solution(mesh):
    field = P("rep", "lev", "tile", None, None, None)
    rows = P("tile", None)
    return jax.shard_map(
        shards,
        mesh=mesh,
        in_specs=(field, rows, rows, P(), field),
        out_specs=(field, field, rows, rows),
        check_vma=False,
    )
```

```python
import functools

import jax
import jax.numpy as jnp
from jax import lax
from jax.experimental import pallas as pl
from jax.experimental.pallas import tpu as pltpu
from jax.sharding import PartitionSpec as P

EPSILON = 1e-05
SCALE = 32 ** (-0.5)
MESH = pl.DeviceIdType.MESH
F32 = jnp.float32
BF16 = jnp.bfloat16
D = 768
HALF = 384
COLS = 4 * HALF
GROUPS = 3
WIDE = COLS // GROUPS
ALONG = (2, 1, -1, 0)
SUM_UP = (0,)
DIRECT_OUT = ()
CHUNK = 48
TOK = 128

BACK = (0, 8, 1, 9)


def dot(a, b):
    return jnp.dot(a, b, preferred_element_type=F32)


def dot_t(a, b):
    return lax.dot_general(a, b, (((1,), (1,)), ((), ())), preferred_element_type=F32)


def t_dot(a, b):
    return lax.dot_general(a, b, (((0,), (0,)), ((), ())), preferred_element_type=F32)


def block_source(block_row, flag):
    group = (block_row >> 4) & 3
    n = block_row & 15
    east = group >> 1
    high = 1 - ((group & 1) ^ (flag * east))
    row = (n >> 2) + 4 * high
    col = (n & 3) + 4 * (1 - east)
    return ((block_row >> 6) << 6) + row * 8 + col


def body(
    tok_hbm, upi_hbm, wq_hbm, wp_hbm, codes_hbm,
    out_hbm, gt_hbm, gqo_hbm, gpo_hbm,
    tok, upi, wq, wp, codes, blocks, win, stage, wsib, wbuf, wnat, hid, ups, hid_t, ups_t, norm, inv_ref,
    qkv, back, mixed, gtok, opart, xs, xr, rsend, rrecv, grad, h2, f2, psum, f1, zs, zr, zo, za,
    out_v, gt_v, gqo_v, gpo_v,
    in_sem, out_sem,
    roll_s, roll_r, w_s, w_r, ga_s, ga_r, gb_s, gb_r, sib_s, sib_r, par_s, par_r, ret_s, ret_r,
    h2_s, h2_r, f2_s, f2_r, f1_s, f1_r, z1_s, z1_r, z2_s, z2_r,
):
    fetched = [
        pltpu.make_async_copy(a, b, in_sem.at[i])
        for i, (a, b) in enumerate(((wq_hbm, wq), (wp_hbm, wp), (codes_hbm, codes), (tok_hbm, tok), (upi_hbm, upi)))
    ]
    for c in fetched:
        c.start()

    rep = lax.axis_index("rep")
    lev = lax.axis_index("lev")
    tile = lax.axis_index("tile")
    core = tile % 2
    chip = tile // 2
    x = chip % 4
    y = chip // 4
    z = lev * 2 + rep
    sib = (rep, lev, chip * 2 + (1 - core))
    p = jnp.where(core == 0, x, y)
    q = jnp.where(core == 0, y, x)
    sp = 1 + 3 * core
    sq = 4 - 3 * core

    def around(value, step):
        return (value + step + 4) % 4

    def at(dp, dq):
        return (rep, lev, (around(p, dp) * sp + around(q, dq) * sq) * 2 + core)

    def at_z(d, where):
        other = (z + d + 8) % 8
        return (other % 2, other // 2, where)

    def near(dz, dt):
        return at_z(dz, (tile + dt + 32) % 32)

    def copy(src, dst, ssem, rsem, where):
        return pltpu.make_async_remote_copy(
            src_ref=src, dst_ref=dst, send_sem=ssem, recv_sem=rsem, device_id=where, device_id_type=MESH
        )

    started = []

    def send(src, dst, ssem, rsem, where):
        c = copy(src, dst, ssem, rsem, where)
        c.start()
        started.append(c)

    def arrived(dst, ssem, rsem):
        copy(dst, dst, ssem, rsem, sib).wait_recv()

    barrier = pltpu.get_barrier_semaphore()
    partners = [sib]
    partners += [at(d, 0) for d in (1, 2, 3)] + [at(0, d) for d in (1, 2, 3)]
    partners += [near(dz, dt) for dz in (1, -1) for dt in (1, -1, 8, -8, 9, -9)]
    partners += [at_z(d, chip * 2 + c) for d in range(1, 8) for c in (0, 1)]
    for partner in partners:
        pl.semaphore_signal(barrier, inc=1, device_id=partner, device_id_type=MESH)

    fetched[0].wait()
    fetched[1].wait()
    for half in range(2):
        for j in range(GROUPS):
            for kind in range(3):
                at_col = kind * D + half * HALF + j * 128
                stage[half, :, j * WIDE + kind * 128:j * WIDE + (kind + 1) * 128] = wq[:, at_col:at_col + 128]
            at_col = half * HALF + j * 128
            stage[half, :, j * WIDE + 384:(j + 1) * WIDE] = wp[:, at_col:at_col + 128]
    for c in fetched[2:]:
        c.wait()
    flag = codes[0, (tile + 31) % 32]
    rows_i = lax.broadcasted_iota(jnp.int32, (TOK, TOK), 0)
    cols_i = lax.broadcasted_iota(jnp.int32, (TOK, TOK), 1)
    order = (cols_i == block_source(rows_i, flag)).astype(F32).astype(BF16)
    blocks[:, :D] = dot(order, tok[...]).astype(BF16)
    blocks[:, D:] = dot(order, upi[...]).astype(BF16)
    pl.semaphore_wait(barrier, len(partners))

    send(stage.at[1 - core], wsib, w_s, w_r, sib)

    def span(level, group):
        return pl.ds(level * 64 + group * 16, 16)

    for group in range(4):
        for level, dz in ((1, 1), (0, -1)):
            n = (1 - level) * 4 + group
            send(blocks.at[span(level, group)], win.at[span(1 - level, group)], roll_s.at[n], roll_r.at[n],
                 near(dz, -BACK[group]))

    arrived(wsib, w_s, w_r)
    mine = stage[core].astype(F32)
    other = wsib[...].astype(F32)
    first = jnp.where(core == 0, mine, other)
    second = jnp.where(core == 0, other, mine)
    chunk = jnp.concatenate([first, second], axis=0).astype(BF16)
    for j in range(GROUPS):
        wbuf[j, q * 4 + p] = chunk[:, j * WIDE:(j + 1) * WIDE]

    def line(buf, j, dq, start=0, count=4):
        return buf.at[j, pl.ds(around(q, dq) * 4 + start, count)]

    def cell(buf, j, dp, dq):
        return buf.at[j, around(q, dq) * 4 + around(p, dp)]

    def gather_first(j):
        own = wbuf.at[j, q * 4 + p]
        for d in (1, 3, 2):
            send(own, own, ga_s.at[j, d], ga_r.at[j, d], at(d, 0))

    def gather_second(j):
        for d in (1, 2, 3):
            arrived(wbuf.at[j, q * 4 + around(p, -d)], ga_s.at[j, d], ga_r.at[j, d])
        send(line(wbuf, j, 0), line(wbuf, j, 0), gb_s.at[j, 0], gb_r.at[j, 0], at(0, 1))
        send(line(wbuf, j, 0), line(wbuf, j, 0), gb_s.at[j, 1], gb_r.at[j, 1], at(0, -1))

    def gather_relay(j):
        arrived(line(wbuf, j, -1), gb_s.at[j, 0], gb_r.at[j, 0])
        send(line(wbuf, j, -1, 0, 2), line(wbuf, j, -1, 0, 2), gb_s.at[j, 2], gb_r.at[j, 2], at(0, 1))
        arrived(line(wbuf, j, 1), gb_s.at[j, 1], gb_r.at[j, 1])
        send(line(wbuf, j, 1, 2, 2), line(wbuf, j, 1, 2, 2), gb_s.at[j, 3], gb_r.at[j, 3], at(0, -1))

    def natural(n):
        return n + core * ((n % 4) * 4 + n // 4 - n)

    def gather_end(j):
        arrived(line(wbuf, j, 2, 0, 2), gb_s.at[j, 2], gb_r.at[j, 2])
        arrived(line(wbuf, j, 2, 2, 2), gb_s.at[j, 3], gb_r.at[j, 3])
        for n in range(16):
            wnat[j, n * CHUNK:(n + 1) * CHUNK, :] = wbuf[j, natural(n)]

    for j in range(GROUPS):
        gather_first(j)
    for j in range(GROUPS):
        gather_second(j)
    gather_relay(0)

    for n in range(8):
        arrived(win.at[pl.ds(n * 16, 16)], roll_s.at[n], roll_r.at[n])
    my_rows = pl.ds(pl.multiple_of(core * TOK, TOK), TOK)
    their_rows = pl.ds(pl.multiple_of((1 - core) * TOK, TOK), TOK)
    ups[my_rows, :] = win[:, D:]
    send(ups.at[my_rows], ups.at[my_rows], sib_s.at[1], sib_r.at[1], sib)
    values = win[:, :D].astype(F32)
    centred = values - jnp.mean(values, axis=1, keepdims=True)
    inverse = lax.rsqrt(jnp.mean(jnp.square(centred), axis=1, keepdims=True) + EPSILON)
    normalized = centred * inverse
    norm[...] = normalized
    inv_ref[...] = jnp.broadcast_to(inverse, (TOK, 128))
    hid[my_rows, :] = normalized.astype(BF16)
    send(hid.at[my_rows], hid.at[my_rows], sib_s.at[0], sib_r.at[0], sib)
    gather_relay(1)
    gather_relay(2)
    arrived(ups.at[their_rows], sib_s.at[1], sib_r.at[1])
    arrived(hid.at[their_rows], sib_s.at[0], sib_r.at[0])
    hid_t[...] = hid[...].T
    ups_t[...] = ups[...].T

    wrapped = jnp.logical_or(z == 0, z == 7)
    allow = jnp.where(wrapped, jnp.where((rows_i >> 6) == (cols_i >> 6), 1.0, 0.0), 1.0).astype(F32)
    allow = jnp.concatenate([allow] * 4, axis=0)
    lane_head = lax.broadcasted_iota(jnp.int32, (TOK, 128), 1) >> 5
    head_masks = [(lane_head == h).astype(F32).astype(BF16) for h in range(4)]

    def stacked(part):
        return jnp.concatenate([part * m for m in head_masks], axis=0)

    def beside(part):
        return jnp.concatenate([part[h * TOK:(h + 1) * TOK] for h in range(4)], axis=1)

    def project(j):
        qkv[...] = dot(hid[...], wnat[j, :, :384]).astype(BF16)
        back[...] = dot(ups[...], wnat[j, :, 384:]).astype(BF16)

    def attend(j):
        for w in range(2):
            rows = slice(w * TOK, (w + 1) * TOK)
            query, key, value = (qkv[rows, kind * 128:(kind + 1) * 128] for kind in range(3))
            coming = back[rows, :]
            query_s, key_s, value_s, coming_s = (stacked(a) for a in (query, key, value, coming))
            raised = jnp.exp(dot_t(query_s, key) * SCALE) * allow
            prob = raised * (1.0 / jnp.sum(raised, axis=1, keepdims=True))
            low = prob.astype(BF16)
            mixed[j, rows, :] = dot(beside(low), value_s).astype(BF16)
            grad_prob = dot_t(coming_s, value)
            centre = jnp.sum(prob * grad_prob, axis=1, keepdims=True)
            grad_scores = (prob * (grad_prob - centre) * SCALE).astype(BF16)
            gtok[j, rows, 0:128] = dot(beside(grad_scores), key_s).astype(BF16)
            gtok[j, rows, 128:256] = t_dot(grad_scores, query_s).astype(BF16)
            gtok[j, rows, 256:384] = t_dot(low, coming_s).astype(BF16)

    def weight_grads(j):
        grad_q = dot(hid_t[...], gtok[j]).astype(BF16)
        grad_p = dot(ups_t[...], mixed[j]).astype(BF16)
        for n in range(16):
            part = slice(n * CHUNK, (n + 1) * CHUNK)
            grad[j, natural(n), :, :384] = grad_q[part]
            grad[j, natural(n), :, 384:] = grad_p[part]

    def outputs_share(j):
        to_output = dot_t(mixed[j], wnat[j, :, 384:])
        to_hidden = dot_t(gtok[j], wnat[j, :, :384])
        if j == 0:
            opart[:, :D] = to_output
            opart[:, D:] = to_hidden
        else:
            opart[:, :D] += to_output
            opart[:, D:] += to_hidden

    def sum_way(j, k, way, dq):
        send(cell(grad, j, ALONG[k], dq), f2.at[j, way, k], f2_s.at[j, way, k], f2_r.at[j, way, k], at(0, dq))

    def sum_start(j):
        for k in range(4):
            if j in DIRECT_OUT:
                for way, dq in ((2, 2), (0, 1), (1, -1)):
                    sum_way(j, k, way, dq)
            else:
                dq = 1 if k in SUM_UP else -1
                send(cell(grad, j, ALONG[k], 2), h2.at[j, k], h2_s.at[j, k], h2_r.at[j, k], at(0, dq))
        if j not in DIRECT_OUT:
            for k in range(4):
                way, dq = (1, -1) if k in SUM_UP else (0, 1)
                sum_way(j, k, way, dq)

    def sum_relay(j):
        if j in DIRECT_OUT:
            return
        for k in range(4):
            way, dq = (0, 1) if k in SUM_UP else (1, -1)
            arrived(h2.at[j, k], h2_s.at[j, k], h2_r.at[j, k])
            place = around(q, dq) * 4 + around(p, ALONG[k])
            grad[j, place] = (grad[j, place].astype(F32) + h2[j, k].astype(F32)).astype(BF16)
            sum_way(j, k, way, dq)

    def sum_first(j):
        for k in range(4):
            total = grad[j, q * 4 + around(p, ALONG[k])].astype(F32)
            for way in (0, 1, 2) if j in DIRECT_OUT else (0, 1):
                arrived(f2.at[j, way, k], f2_s.at[j, way, k], f2_r.at[j, way, k])
                total = total + f2[j, way, k].astype(F32)
            psum[j, k] = total.astype(BF16)
            if k < 3:
                d = (2, 1, 3)[k]
                send(psum.at[j, k], f1.at[j, d], f1_s.at[j, d], f1_r.at[j, d], at(d, 0))

    def sum_z(j):
        total = psum[j, 3].astype(F32)
        for d in (1, 3, 2):
            arrived(f1.at[j, d], f1_s.at[j, d], f1_r.at[j, d])
            total = total + f1[j, d].astype(F32)
        for kind in range(4):
            for r in range(2):
                zs[j, kind * 2 + r] = total[r * 24:(r + 1) * 24, kind * 128:(kind + 1) * 128].astype(BF16)
        for d in (4, 3, 5, 2, 6, 1, 7):
            send(zs.at[j, (z + d) % 8], zr.at[j, d], z1_s.at[j, d], z1_r.at[j, d], at_z(d, chip * 2 + core))

    half_here = z % 2
    slot = (z // 2) * 2 + core
    to_sibling = []

    def hand_out(j):
        total = zs[j, z].astype(F32)
        for d in range(1, 8):
            arrived(zr.at[j, d], z1_s.at[j, d], z1_r.at[j, d])
            total = total + zr[j, d].astype(F32)
        zo[j] = total.astype(BF16)
        for d in (4, 3, 5, 2, 6, 1, 7):
            send(zo.at[j], za.at[j, slot], z2_s.at[j, d], z2_r.at[j, slot], at_z(d, chip * 2 + half_here))
        here = copy(zo.at[j], za.at[j, slot], z2_s.at[j, 0], z2_r.at[j, slot], sib)
        to_sibling.append(here)

        @pl.when(half_here == core)
        def _():
            za[j, slot] = zo[j]

        @pl.when(half_here != core)
        def _():
            here.start()

    def finish(j):
        for n in range(8):
            own = jnp.logical_and(half_here == core, slot == n)

            @pl.when(jnp.logical_not(own))
            def _():
                arrived(za.at[j, n], z2_s.at[j, 0], z2_r.at[j, n])
        for kind in range(4):
            for half in range(2):
                piece = za[j, kind * 2 + half].astype(F32)
                at_col = half * HALF + j * 128
                if kind < 3:
                    gqo_v[:, kind * D + at_col:kind * D + at_col + 128] = piece
                else:
                    gpo_v[:, at_col:at_col + 128] = piece

    def give_back():
        arrived(xr, par_s, par_r)
        total = win[:, :D].astype(F32) + opart[my_rows, :D] + xr[:, :D].astype(F32)
        rsend[:, :D] = total.astype(BF16)
        grad_hidden = opart[my_rows, D:] + xr[:, D:].astype(F32)
        normalized = norm[...]
        centre = jnp.mean(grad_hidden, axis=1, keepdims=True)
        along_norm = jnp.mean(grad_hidden * normalized, axis=1, keepdims=True)
        moved = (grad_hidden - centre - normalized * along_norm) * inv_ref[:, :1]
        rsend[:, D:] = (win[:, D:].astype(F32) + moved).astype(BF16)
        for group in range(4):
            for level, dz in ((1, -1), (0, 1)):
                n = level * 4 + group
                send(rsend.at[span(1 - level, group)], rrecv.at[span(level, group)], ret_s.at[n], ret_r.at[n],
                     near(dz, BACK[group]))

    gather_end(0)
    project(0)
    attend(0)
    weight_grads(0)
    sum_start(0)
    gather_end(1)
    project(1)
    attend(1)
    weight_grads(1)
    sum_start(1)
    sum_relay(0)
    gather_end(2)
    project(2)
    attend(2)
    weight_grads(2)
    sum_start(2)
    outputs_share(0)
    outputs_share(1)
    outputs_share(2)
    xs[...] = opart[their_rows, :].astype(BF16)
    send(xs, xr, par_s, par_r, sib)
    sum_relay(1)
    sum_first(0)
    sum_relay(2)
    give_back()
    sum_z(0)
    sum_first(1)
    sum_first(2)
    hand_out(0)
    sum_z(1)
    sum_z(2)
    hand_out(1)

    for n in range(8):
        arrived(rrecv.at[pl.ds(n * 16, 16)], ret_s.at[n], ret_r.at[n])
    order_t = (rows_i == block_source(cols_i, flag)).astype(F32).astype(BF16)
    out_v[...] = dot(order_t, rrecv[:, :D]).astype(BF16)
    gt_v[...] = dot(order_t, rrecv[:, D:]).astype(BF16)
    written = [
        pltpu.make_async_copy(a, b, out_sem.at[i])
        for i, (a, b) in enumerate(((out_v, out_hbm), (gt_v, gt_hbm), (gqo_v, gqo_hbm), (gpo_v, gpo_hbm)))
    ]
    written[0].start()
    written[1].start()
    finish(0)
    hand_out(2)
    finish(1)
    finish(2)
    written[2].start()
    written[3].start()
    for c in started:
        c.wait_send()

    @pl.when(half_here != core)
    def _():
        for c in to_sibling:
            c.wait_send()

    for c in written:
        c.wait()


def place_body(*refs):
    ins, outs, held, sem = refs[:4], refs[4:8], refs[8:12], refs[12]
    reads = [pltpu.make_async_copy(a, b, sem.at[0, i]) for i, (a, b) in enumerate(zip(ins, held))]
    writes = [pltpu.make_async_copy(a, b, sem.at[1, i]) for i, (a, b) in enumerate(zip(held, outs))]
    for c in reads:
        c.start()
    for r, w in zip(reads, writes):
        r.wait()
        w.start()
    for c in writes:
        c.wait()


def shards(tokens, w_qkv, w_proj, seam_codes, upstream):
    dma = pltpu.SemaphoreType.DMA
    vmem = pltpu.VMEM
    scratch = [
        vmem((TOK, D), BF16),
        vmem((TOK, D), BF16),
        vmem((24, 3 * D), BF16),
        vmem((24, D), BF16),
        pltpu.SMEM((2, 32), jnp.int32),
        vmem((TOK, 2 * D), BF16),
        vmem((TOK, 2 * D), BF16),
        vmem((2, 24, COLS), BF16),
        vmem((24, COLS), BF16),
        vmem((GROUPS, 16, CHUNK, WIDE), BF16),
        vmem((GROUPS, D, WIDE), BF16),
        vmem((2 * TOK, D), BF16),
        vmem((2 * TOK, D), BF16),
        vmem((D, 2 * TOK), BF16),
        vmem((D, 2 * TOK), BF16),
        vmem((TOK, D), F32),
        vmem((TOK, 128), F32),
        vmem((2 * TOK, 384), BF16),
        vmem((2 * TOK, 128), BF16),
        vmem((GROUPS, 2 * TOK, 128), BF16),
        vmem((GROUPS, 2 * TOK, 384), BF16),
        vmem((2 * TOK, 2 * D), F32),
        vmem((TOK, 2 * D), BF16),
        vmem((TOK, 2 * D), BF16),
        vmem((TOK, 2 * D), BF16),
        vmem((TOK, 2 * D), BF16),
        vmem((GROUPS, 16, CHUNK, WIDE), BF16),
        vmem((GROUPS, 4, CHUNK, WIDE), BF16),
        vmem((GROUPS, 3, 4, CHUNK, WIDE), BF16),
        vmem((GROUPS, 4, CHUNK, WIDE), BF16),
        vmem((GROUPS, 4, CHUNK, WIDE), BF16),
        vmem((GROUPS, 8, 24, 128), BF16),
        vmem((GROUPS, 8, 24, 128), BF16),
        vmem((GROUPS, 24, 128), BF16),
        vmem((GROUPS, 8, 24, 128), BF16),
        vmem((TOK, D), BF16),
        vmem((TOK, D), BF16),
        vmem((24, 3 * D), F32),
        vmem((24, D), F32),
        dma((5,)), dma((4,)),
        dma((8,)), dma((8,)),
        dma, dma,
        dma((GROUPS, 4)), dma((GROUPS, 4)),
        dma((GROUPS, 4)), dma((GROUPS, 4)),
        dma((2,)), dma((2,)),
        dma, dma,
        dma((8,)), dma((8,)),
        dma((GROUPS, 4)), dma((GROUPS, 4)),
        dma((GROUPS, 3, 4)), dma((GROUPS, 3, 4)),
        dma((GROUPS, 4)), dma((GROUPS, 4)),
        dma((GROUPS, 8)), dma((GROUPS, 8)), dma((GROUPS, 8)), dma((GROUPS, 8)),
    ]
    anywhere = pl.BlockSpec(memory_space=pl.ANY)
    shapes = (
        jax.ShapeDtypeStruct((TOK, D), BF16),
        jax.ShapeDtypeStruct((TOK, D), BF16),
        jax.ShapeDtypeStruct((24, 3 * D), F32),
        jax.ShapeDtypeStruct((24, D), F32),
    )
    results = pl.pallas_call(
        body,
        out_shape=shapes,
        in_specs=[anywhere] * 5,
        out_specs=(anywhere,) * 4,
        scratch_shapes=scratch,
        compiler_params=pltpu.CompilerParams(
            collective_id=0, has_side_effects=True, vmem_limit_bytes=56 * 1024 * 1024
        ),
        name="layer",
    )(tokens.reshape(TOK, D), upstream.reshape(TOK, D), w_qkv, w_proj, seam_codes.T)
    out, grad_tok, grad_qkv, grad_proj = pl.pallas_call(
        place_body,
        out_shape=shapes,
        in_specs=[anywhere] * 4,
        out_specs=(anywhere,) * 4,
        scratch_shapes=[vmem(a.shape, a.dtype) for a in shapes] + [dma((2, 4))],
        name="place",
    )(*results)
    return (out.reshape(tokens.shape), grad_tok.reshape(tokens.shape), grad_qkv, grad_proj)


def solution(mesh):
    field = P("rep", "lev", "tile", None, None, None)
    rows = P("tile", None)
    return jax.shard_map(
        shards,
        mesh=mesh,
        in_specs=(field, rows, rows, P(), field),
        out_specs=(field, field, rows, rows),
        check_vma=False,
    )
```

```python
import functools

import jax
import jax.numpy as jnp
from jax import lax
from jax.experimental import pallas as pl
from jax.experimental.pallas import tpu as pltpu
from jax.sharding import PartitionSpec as P

EPSILON = 1e-05
SCALE = 32 ** (-0.5)
MESH = pl.DeviceIdType.MESH
F32 = jnp.float32
BF16 = jnp.bfloat16
D = 768
HALF = 384
COLS = 4 * HALF
GROUPS = 3
WIDE = COLS // GROUPS
ALONG = (2, 1, -1, 0)
SUM_UP = (0,)
DIRECT_OUT = ()
CHUNK = 48
TOK = 128

BACK = (0, 8, 1, 9)


def dot(a, b):
    return jnp.dot(a, b, preferred_element_type=F32)


def dot_t(a, b):
    return lax.dot_general(a, b, (((1,), (1,)), ((), ())), preferred_element_type=F32)


def t_dot(a, b):
    return lax.dot_general(a, b, (((0,), (0,)), ((), ())), preferred_element_type=F32)


def block_source(block_row, flag):
    group = (block_row >> 4) & 3
    n = block_row & 15
    east = group >> 1
    high = 1 - ((group & 1) ^ (flag * east))
    row = (n >> 2) + 4 * high
    col = (n & 3) + 4 * (1 - east)
    return ((block_row >> 6) << 6) + row * 8 + col


def body(
    tok_hbm, upi_hbm, wq_hbm, wp_hbm, codes_hbm,
    out_hbm, gt_hbm, za,
    tok, upi, wq, wp, codes, blocks, win, stage, wout, wsib, wbuf, wnat, hid, ups, hid_t, ups_t, norm, inv_ref,
    qkv, back, mixed, gtok, opart, xs, xr, rsend, rrecv, grad, h2, f2, psum, f1, zs, zr, zo,
    out_v, gt_v,
    in_sem, out_sem, own_sem,
    roll_s, roll_r, w_s, w_r, ga_s, ga_r, gb_s, gb_r, sib_s, sib_r, par_s, par_r, ret_s, ret_r,
    h2_s, h2_r, f2_s, f2_r, f1_s, f1_r, z1_s, z1_r, z2_s, z2_r,
):
    fetched = [
        pltpu.make_async_copy(a, b, in_sem.at[i])
        for i, (a, b) in enumerate(((wq_hbm, wq), (wp_hbm, wp), (codes_hbm, codes), (tok_hbm, tok), (upi_hbm, upi)))
    ]
    for c in fetched:
        c.start()

    rep = lax.axis_index("rep")
    lev = lax.axis_index("lev")
    tile = lax.axis_index("tile")
    core = tile % 2
    chip = tile // 2
    x = chip % 4
    y = chip // 4
    z = lev * 2 + rep
    sib = (rep, lev, chip * 2 + (1 - core))
    p = jnp.where(core == 0, x, y)
    q = jnp.where(core == 0, y, x)
    sp = 1 + 3 * core
    sq = 4 - 3 * core

    def around(value, step):
        return (value + step + 4) % 4

    def at(dp, dq):
        return (rep, lev, (around(p, dp) * sp + around(q, dq) * sq) * 2 + core)

    def at_z(d, where):
        other = (z + d + 8) % 8
        return (other % 2, other // 2, where)

    def near(dz, dt):
        return at_z(dz, (tile + dt + 32) % 32)

    def copy(src, dst, ssem, rsem, where):
        return pltpu.make_async_remote_copy(
            src_ref=src, dst_ref=dst, send_sem=ssem, recv_sem=rsem, device_id=where, device_id_type=MESH
        )

    started = []

    def send(src, dst, ssem, rsem, where):
        c = copy(src, dst, ssem, rsem, where)
        c.start()
        started.append(c)

    def arrived(dst, ssem, rsem):
        copy(dst, dst, ssem, rsem, sib).wait_recv()

    barrier = pltpu.get_barrier_semaphore()
    partners = [sib]
    partners += [at(d, 0) for d in (1, 2, 3)] + [at(0, d) for d in (1, 2, 3)]
    partners += [near(dz, dt) for dz in (1, -1) for dt in (1, -1, 8, -8, 9, -9)]
    partners += [at_z(d, chip * 2 + c) for d in range(1, 8) for c in (0, 1)]
    for partner in partners:
        pl.semaphore_signal(barrier, inc=1, device_id=partner, device_id_type=MESH)

    fetched[0].wait()
    fetched[1].wait()
    for half in range(2):
        for j in range(GROUPS):
            for kind in range(3):
                at_col = kind * D + half * HALF + j * 128
                stage[half, :, j * WIDE + kind * 128:j * WIDE + (kind + 1) * 128] = wq[:, at_col:at_col + 128]
            at_col = half * HALF + j * 128
            stage[half, :, j * WIDE + 384:(j + 1) * WIDE] = wp[:, at_col:at_col + 128]
    for c in fetched[2:]:
        c.wait()
    flag = codes[0, (tile + 31) % 32]
    rows_i = lax.broadcasted_iota(jnp.int32, (TOK, TOK), 0)
    cols_i = lax.broadcasted_iota(jnp.int32, (TOK, TOK), 1)
    order = (cols_i == block_source(rows_i, flag)).astype(F32).astype(BF16)
    blocks[:, :D] = dot(order, tok[...]).astype(BF16)
    blocks[:, D:] = dot(order, upi[...]).astype(BF16)
    leaving = stage[1 - core].astype(F32)
    wout[...] = jnp.concatenate([leaving[:, :D], leaving[:, D:]], axis=0).astype(BF16)
    pl.semaphore_wait(barrier, len(partners))

    send(wout, wsib, w_s, w_r, sib)

    def span(level, group):
        return pl.ds(level * 64 + group * 16, 16)

    for group in range(4):
        for level, dz in ((1, 1), (0, -1)):
            n = (1 - level) * 4 + group
            send(blocks.at[span(level, group)], win.at[span(1 - level, group)], roll_s.at[n], roll_r.at[n],
                 near(dz, -BACK[group]))

    arrived(wsib, w_s, w_r)
    mine = stage[core].astype(F32)
    other = wsib[...].astype(F32)
    other = jnp.concatenate([other[:24], other[24:]], axis=1)
    first = jnp.where(core == 0, mine, other)
    second = jnp.where(core == 0, other, mine)
    chunk = jnp.concatenate([first, second], axis=0).astype(BF16)
    for j in range(GROUPS):
        wbuf[j, q * 4 + p] = chunk[:, j * WIDE:(j + 1) * WIDE]

    def line(buf, j, dq, start=0, count=4):
        return buf.at[j, pl.ds(around(q, dq) * 4 + start, count)]

    def cell(buf, j, dp, dq):
        return buf.at[j, around(q, dq) * 4 + around(p, dp)]

    def gather_first(j):
        own = wbuf.at[j, q * 4 + p]
        for d in (1, 3, 2):
            send(own, own, ga_s.at[j, d], ga_r.at[j, d], at(d, 0))

    def gather_second(j):
        for d in (1, 2, 3):
            arrived(wbuf.at[j, q * 4 + around(p, -d)], ga_s.at[j, d], ga_r.at[j, d])
        send(line(wbuf, j, 0), line(wbuf, j, 0), gb_s.at[j, 0], gb_r.at[j, 0], at(0, 1))
        send(line(wbuf, j, 0), line(wbuf, j, 0), gb_s.at[j, 1], gb_r.at[j, 1], at(0, -1))

    def gather_relay(j):
        arrived(line(wbuf, j, -1), gb_s.at[j, 0], gb_r.at[j, 0])
        send(line(wbuf, j, -1, 0, 3), line(wbuf, j, -1, 0, 3), gb_s.at[j, 2], gb_r.at[j, 2], at(0, 1))
        arrived(line(wbuf, j, 1), gb_s.at[j, 1], gb_r.at[j, 1])
        send(line(wbuf, j, 1, 3, 1), line(wbuf, j, 1, 3, 1), gb_s.at[j, 3], gb_r.at[j, 3], at(0, -1))

    def natural(n):
        return n + core * ((n % 4) * 4 + n // 4 - n)

    def gather_end(j):
        arrived(line(wbuf, j, 2, 0, 3), gb_s.at[j, 2], gb_r.at[j, 2])
        arrived(line(wbuf, j, 2, 3, 1), gb_s.at[j, 3], gb_r.at[j, 3])
        for n in range(16):
            wnat[j, n * CHUNK:(n + 1) * CHUNK, :] = wbuf[j, natural(n)]

    for j in range(GROUPS):
        gather_first(j)
    for j in range(GROUPS):
        gather_second(j)
    gather_relay(0)

    for n in range(8):
        arrived(win.at[pl.ds(n * 16, 16)], roll_s.at[n], roll_r.at[n])
    my_rows = pl.ds(pl.multiple_of(core * TOK, TOK), TOK)
    their_rows = pl.ds(pl.multiple_of((1 - core) * TOK, TOK), TOK)
    ups[my_rows, :] = win[:, D:]
    send(ups.at[my_rows], ups.at[my_rows], sib_s.at[1], sib_r.at[1], sib)
    values = win[:, :D].astype(F32)
    centred = values - jnp.mean(values, axis=1, keepdims=True)
    inverse = lax.rsqrt(jnp.mean(jnp.square(centred), axis=1, keepdims=True) + EPSILON)
    normalized = centred * inverse
    norm[...] = normalized
    inv_ref[...] = jnp.broadcast_to(inverse, (TOK, 128))
    hid[my_rows, :] = normalized.astype(BF16)
    send(hid.at[my_rows], hid.at[my_rows], sib_s.at[0], sib_r.at[0], sib)
    gather_relay(1)
    gather_relay(2)
    arrived(ups.at[their_rows], sib_s.at[1], sib_r.at[1])
    arrived(hid.at[their_rows], sib_s.at[0], sib_r.at[0])
    hid_t[...] = hid[...].T
    ups_t[...] = ups[...].T

    wrapped = jnp.logical_or(z == 0, z == 7)
    allow = jnp.where(wrapped, jnp.where((rows_i >> 6) == (cols_i >> 6), 1.0, 0.0), 1.0).astype(F32)
    allow = jnp.concatenate([allow] * 4, axis=0)
    lane_head = lax.broadcasted_iota(jnp.int32, (TOK, 128), 1) >> 5
    head_masks = [(lane_head == h).astype(F32).astype(BF16) for h in range(4)]

    def stacked(part):
        return jnp.concatenate([part * m for m in head_masks], axis=0)

    def beside(part):
        return jnp.concatenate([part[h * TOK:(h + 1) * TOK] for h in range(4)], axis=1)

    def project(j):
        qkv[...] = dot(hid[...], wnat[j, :, :384]).astype(BF16)
        back[...] = dot(ups[...], wnat[j, :, 384:]).astype(BF16)

    def attend(j):
        for w in range(2):
            rows = slice(w * TOK, (w + 1) * TOK)
            query, key, value = (qkv[rows, kind * 128:(kind + 1) * 128] for kind in range(3))
            coming = back[rows, :]
            query_s, key_s, value_s, coming_s = (stacked(a) for a in (query, key, value, coming))
            raised = jnp.exp(dot_t(query_s, key) * SCALE) * allow
            prob = raised * (1.0 / jnp.sum(raised, axis=1, keepdims=True))
            low = prob.astype(BF16)
            mixed[j, rows, :] = dot(beside(low), value_s).astype(BF16)
            grad_prob = dot_t(coming_s, value)
            centre = jnp.sum(prob * grad_prob, axis=1, keepdims=True)
            grad_scores = (prob * (grad_prob - centre) * SCALE).astype(BF16)
            gtok[j, rows, 0:128] = dot(beside(grad_scores), key_s).astype(BF16)
            gtok[j, rows, 128:256] = t_dot(grad_scores, query_s).astype(BF16)
            gtok[j, rows, 256:384] = t_dot(low, coming_s).astype(BF16)

    def weight_grads(j):
        grad_q = dot(hid_t[...], gtok[j]).astype(BF16)
        grad_p = dot(ups_t[...], mixed[j]).astype(BF16)
        for n in range(16):
            part = slice(n * CHUNK, (n + 1) * CHUNK)
            grad[j, natural(n), :, :384] = grad_q[part]
            grad[j, natural(n), :, 384:] = grad_p[part]

    def outputs_share(j):
        to_output = dot_t(mixed[j], wnat[j, :, 384:])
        to_hidden = dot_t(gtok[j], wnat[j, :, :384])
        if j == 0:
            opart[:, :D] = to_output
            opart[:, D:] = to_hidden
        else:
            opart[:, :D] += to_output
            opart[:, D:] += to_hidden

    def sum_way(j, k, way, dq):
        send(cell(grad, j, ALONG[k], dq), f2.at[j, way, k], f2_s.at[j, way, k], f2_r.at[j, way, k], at(0, dq))

    def sum_start(j):
        for k in range(4):
            if j in DIRECT_OUT:
                for way, dq in ((2, 2), (0, 1), (1, -1)):
                    sum_way(j, k, way, dq)
            else:
                dq = 1 if k in SUM_UP else -1
                send(cell(grad, j, ALONG[k], 2), h2.at[j, k], h2_s.at[j, k], h2_r.at[j, k], at(0, dq))
        if j not in DIRECT_OUT:
            for k in range(4):
                way, dq = (1, -1) if k in SUM_UP else (0, 1)
                sum_way(j, k, way, dq)

    def sum_relay(j):
        if j in DIRECT_OUT:
            return
        for k in range(4):
            way, dq = (0, 1) if k in SUM_UP else (1, -1)
            arrived(h2.at[j, k], h2_s.at[j, k], h2_r.at[j, k])
            place = around(q, dq) * 4 + around(p, ALONG[k])
            grad[j, place] = (grad[j, place].astype(F32) + h2[j, k].astype(F32)).astype(BF16)
            sum_way(j, k, way, dq)

    def sum_first(j):
        for k in range(4):
            total = grad[j, q * 4 + around(p, ALONG[k])].astype(F32)
            for way in (0, 1, 2) if j in DIRECT_OUT else (0, 1):
                arrived(f2.at[j, way, k], f2_s.at[j, way, k], f2_r.at[j, way, k])
                total = total + f2[j, way, k].astype(F32)
            psum[j, k] = total.astype(BF16)
            if k < 3:
                d = (2, 1, 3)[k]
                send(psum.at[j, k], f1.at[j, d], f1_s.at[j, d], f1_r.at[j, d], at(d, 0))

    def sum_z(j):
        total = psum[j, 3].astype(F32)
        for d in (1, 3, 2):
            arrived(f1.at[j, d], f1_s.at[j, d], f1_r.at[j, d])
            total = total + f1[j, d].astype(F32)
        for kind in range(4):
            for r in range(2):
                zs[j, kind * 2 + r] = total[r * 24:(r + 1) * 24, kind * 128:(kind + 1) * 128].astype(BF16)
        for d in (4, 3, 5, 2, 6, 1, 7):
            send(zs.at[j, (z + d) % 8], zr.at[j, d], z1_s.at[j, d], z1_r.at[j, d], at_z(d, chip * 2 + core))

    half_here = z % 2
    slot = (z // 2) * 2 + core
    to_sibling = []

    def hand_out(j):
        total = zs[j, z].astype(F32)
        for d in range(1, 8):
            arrived(zr.at[j, d], z1_s.at[j, d], z1_r.at[j, d])
            total = total + zr[j, d].astype(F32)
        zo[j] = total.astype(BF16)
        for d in (4, 3, 5, 2, 6, 1, 7):
            send(zo.at[j], za.at[j, slot], z2_s.at[j, d], z2_r.at[j, slot], at_z(d, chip * 2 + half_here))
        here = copy(zo.at[j], za.at[j, slot], z2_s.at[j, 0], z2_r.at[j, slot], sib)
        to_sibling.append(here)

        @pl.when(half_here == core)
        def _():
            pltpu.make_async_copy(zo.at[j], za.at[j, slot], own_sem.at[j]).start()

        @pl.when(half_here != core)
        def _():
            here.start()

    def finish(j):
        for n in range(8):
            own = jnp.logical_and(half_here == core, slot == n)

            @pl.when(jnp.logical_not(own))
            def _():
                arrived(za.at[j, n], z2_s.at[j, 0], z2_r.at[j, n])

        @pl.when(half_here == core)
        def _():
            pltpu.make_async_copy(zo.at[j], za.at[j, slot], own_sem.at[j]).wait()

    def give_back():
        arrived(xr, par_s, par_r)
        total = win[:, :D].astype(F32) + opart[my_rows, :D] + xr[:, :D].astype(F32)
        rsend[:, :D] = total.astype(BF16)
        grad_hidden = opart[my_rows, D:] + xr[:, D:].astype(F32)
        normalized = norm[...]
        centre = jnp.mean(grad_hidden, axis=1, keepdims=True)
        along_norm = jnp.mean(grad_hidden * normalized, axis=1, keepdims=True)
        moved = (grad_hidden - centre - normalized * along_norm) * inv_ref[:, :1]
        rsend[:, D:] = (win[:, D:].astype(F32) + moved).astype(BF16)
        for group in range(4):
            for level, dz in ((1, -1), (0, 1)):
                n = level * 4 + group
                send(rsend.at[span(1 - level, group)], rrecv.at[span(level, group)], ret_s.at[n], ret_r.at[n],
                     near(dz, BACK[group]))

    gather_end(0)
    project(0)
    attend(0)
    weight_grads(0)
    sum_start(0)
    gather_end(1)
    project(1)
    attend(1)
    weight_grads(1)
    sum_start(1)
    sum_relay(0)
    gather_end(2)
    project(2)
    attend(2)
    weight_grads(2)
    sum_start(2)
    outputs_share(0)
    sum_relay(1)
    outputs_share(1)
    outputs_share(2)
    xs[...] = opart[their_rows, :].astype(BF16)
    send(xs, xr, par_s, par_r, sib)
    sum_first(0)
    sum_relay(2)
    give_back()
    sum_z(0)
    sum_first(1)
    sum_first(2)
    hand_out(0)
    sum_z(1)
    sum_z(2)
    hand_out(1)

    for n in range(8):
        arrived(rrecv.at[pl.ds(n * 16, 16)], ret_s.at[n], ret_r.at[n])
    order_t = (rows_i == block_source(cols_i, flag)).astype(F32).astype(BF16)
    out_v[...] = dot(order_t, rrecv[:, :D]).astype(BF16)
    gt_v[...] = dot(order_t, rrecv[:, D:]).astype(BF16)
    written = [
        pltpu.make_async_copy(a, b, out_sem.at[i])
        for i, (a, b) in enumerate(((out_v, out_hbm), (gt_v, gt_hbm)))
    ]
    written[0].start()
    written[1].start()
    finish(0)
    hand_out(2)
    finish(1)
    finish(2)
    for c in started:
        c.wait_send()

    @pl.when(half_here != core)
    def _():
        for c in to_sibling:
            c.wait_send()

    for c in written:
        c.wait()


def place_body(out_a, gt_a, za_a, out_b, gt_b, gq_b, gp_b, out_v, gt_v, za_v, gq_v, gp_v, sem):
    reads = [
        pltpu.make_async_copy(a, b, sem.at[0, i]) for i, (a, b) in enumerate(((za_a, za_v), (out_a, out_v), (gt_a, gt_v)))
    ]
    writes = [
        pltpu.make_async_copy(a, b, sem.at[1, i])
        for i, (a, b) in enumerate(((gq_v, gq_b), (gp_v, gp_b), (out_v, out_b), (gt_v, gt_b)))
    ]
    for c in reads:
        c.start()
    reads[0].wait()
    for kind in range(4):
        for j in range(GROUPS):
            for half in range(2):
                piece = za_v[j, kind * 2 + half].astype(F32)
                at_col = half * HALF + j * 128
                if kind < 3:
                    gq_v[:, kind * D + at_col:kind * D + at_col + 128] = piece
                else:
                    gp_v[:, at_col:at_col + 128] = piece
    writes[0].start()
    writes[1].start()
    for k in (1, 2):
        reads[k].wait()
        writes[k + 1].start()
    for c in writes:
        c.wait()


def shards(tokens, w_qkv, w_proj, seam_codes, upstream):
    dma = pltpu.SemaphoreType.DMA
    vmem = pltpu.VMEM
    scratch = [
        vmem((TOK, D), BF16),
        vmem((TOK, D), BF16),
        vmem((24, 3 * D), BF16),
        vmem((24, D), BF16),
        pltpu.SMEM((2, 32), jnp.int32),
        vmem((TOK, 2 * D), BF16),
        vmem((TOK, 2 * D), BF16),
        vmem((2, 24, COLS), BF16),
        vmem((48, D), BF16),
        vmem((48, D), BF16),
        vmem((GROUPS, 16, CHUNK, WIDE), BF16),
        vmem((GROUPS, D, WIDE), BF16),
        vmem((2 * TOK, D), BF16),
        vmem((2 * TOK, D), BF16),
        vmem((D, 2 * TOK), BF16),
        vmem((D, 2 * TOK), BF16),
        vmem((TOK, D), F32),
        vmem((TOK, 128), F32),
        vmem((2 * TOK, 384), BF16),
        vmem((2 * TOK, 128), BF16),
        vmem((GROUPS, 2 * TOK, 128), BF16),
        vmem((GROUPS, 2 * TOK, 384), BF16),
        vmem((2 * TOK, 2 * D), F32),
        vmem((TOK, 2 * D), BF16),
        vmem((TOK, 2 * D), BF16),
        vmem((TOK, 2 * D), BF16),
        vmem((TOK, 2 * D), BF16),
        vmem((GROUPS, 16, CHUNK, WIDE), BF16),
        vmem((GROUPS, 4, CHUNK, WIDE), BF16),
        vmem((GROUPS, 3, 4, CHUNK, WIDE), BF16),
        vmem((GROUPS, 4, CHUNK, WIDE), BF16),
        vmem((GROUPS, 4, CHUNK, WIDE), BF16),
        vmem((GROUPS, 8, 24, 128), BF16),
        vmem((GROUPS, 8, 24, 128), BF16),
        vmem((GROUPS, 24, 128), BF16),
        vmem((TOK, D), BF16),
        vmem((TOK, D), BF16),
        dma((5,)), dma((2,)), dma((GROUPS,)),
        dma((8,)), dma((8,)),
        dma, dma,
        dma((GROUPS, 4)), dma((GROUPS, 4)),
        dma((GROUPS, 4)), dma((GROUPS, 4)),
        dma((2,)), dma((2,)),
        dma, dma,
        dma((8,)), dma((8,)),
        dma((GROUPS, 4)), dma((GROUPS, 4)),
        dma((GROUPS, 3, 4)), dma((GROUPS, 3, 4)),
        dma((GROUPS, 4)), dma((GROUPS, 4)),
        dma((GROUPS, 8)), dma((GROUPS, 8)), dma((GROUPS, 8)), dma((GROUPS, 8)),
    ]
    anywhere = pl.BlockSpec(memory_space=pl.ANY)
    shapes = (
        jax.ShapeDtypeStruct((TOK, D), BF16),
        jax.ShapeDtypeStruct((TOK, D), BF16),
        jax.ShapeDtypeStruct((24, 3 * D), F32),
        jax.ShapeDtypeStruct((24, D), F32),
    )
    pieces = jax.ShapeDtypeStruct((GROUPS, 8, 24, 128), BF16)
    results = pl.pallas_call(
        body,
        out_shape=shapes[:2] + (pieces,),
        in_specs=[anywhere] * 5,
        out_specs=(anywhere,) * 3,
        scratch_shapes=scratch,
        compiler_params=pltpu.CompilerParams(
            collective_id=0, has_side_effects=True, vmem_limit_bytes=56 * 1024 * 1024
        ),
        name="layer",
    )(tokens.reshape(TOK, D), upstream.reshape(TOK, D), w_qkv, w_proj, seam_codes.T)
    out, grad_tok, grad_qkv, grad_proj = pl.pallas_call(
        place_body,
        out_shape=shapes,
        in_specs=[anywhere] * 3,
        out_specs=(anywhere,) * 4,
        scratch_shapes=[vmem(a.shape, a.dtype) for a in shapes[:2] + (pieces,) + shapes[2:]] + [dma((2, 4))],
        name="place",
    )(*results)
    return (out.reshape(tokens.shape), grad_tok.reshape(tokens.shape), grad_qkv, grad_proj)


def solution(mesh):
    field = P("rep", "lev", "tile", None, None, None)
    rows = P("tile", None)
    return jax.shard_map(
        shards,
        mesh=mesh,
        in_specs=(field, rows, rows, P(), field),
        out_specs=(field, field, rows, rows),
        check_vma=False,
    )
```

```python
import functools

import jax
import jax.numpy as jnp
from jax import lax
from jax.experimental import pallas as pl
from jax.experimental.pallas import tpu as pltpu
from jax.sharding import PartitionSpec as P

EPSILON = 1e-05
SCALE = 32 ** (-0.5)
MESH = pl.DeviceIdType.MESH
F32 = jnp.float32
BF16 = jnp.bfloat16
D = 768
HALF = 384
COLS = 4 * HALF
GROUPS = 3
WIDE = COLS // GROUPS
ALONG = (2, 1, -1, 0)
SUM_UP = (0,)
DIRECT_OUT = ()
CHUNK = 48
TOK = 128

BACK = (0, 8, 1, 9)


def dot(a, b):
    return jnp.dot(a, b, preferred_element_type=F32)


def dot_t(a, b):
    return lax.dot_general(a, b, (((1,), (1,)), ((), ())), preferred_element_type=F32)


def t_dot(a, b):
    return lax.dot_general(a, b, (((0,), (0,)), ((), ())), preferred_element_type=F32)


def block_source(block_row, flag):
    group = (block_row >> 4) & 3
    n = block_row & 15
    east = group >> 1
    high = 1 - ((group & 1) ^ (flag * east))
    row = (n >> 2) + 4 * high
    col = (n & 3) + 4 * (1 - east)
    return ((block_row >> 6) << 6) + row * 8 + col


def body(
    tok_hbm, upi_hbm, wq_hbm, wp_hbm, codes_hbm,
    out_hbm, gt_hbm, za,
    tok, upi, wq, wp, codes, blocks, win, stage, wout, wsib, wbuf, wnat, hid, ups, hid_t, ups_t, norm, inv_ref,
    qkv, back, mixed, gtok, opart, xs, xr, rsend, rrecv, grad, h2, f2, psum, f1, zs, zr, zo,
    out_v, gt_v,
    in_sem, out_sem, own_sem,
    roll_s, roll_r, w_s, w_r, ga_s, ga_r, gb_s, gb_r, sib_s, sib_r, par_s, par_r, ret_s, ret_r,
    h2_s, h2_r, f2_s, f2_r, f1_s, f1_r, z1_s, z1_r, z2_s, z2_r,
):
    fetched = [
        pltpu.make_async_copy(a, b, in_sem.at[i])
        for i, (a, b) in enumerate(((wq_hbm, wq), (wp_hbm, wp), (codes_hbm, codes), (tok_hbm, tok), (upi_hbm, upi)))
    ]
    for c in fetched:
        c.start()

    rep = lax.axis_index("rep")
    lev = lax.axis_index("lev")
    tile = lax.axis_index("tile")
    core = tile % 2
    chip = tile // 2
    x = chip % 4
    y = chip // 4
    z = lev * 2 + rep
    sib = (rep, lev, chip * 2 + (1 - core))
    p = jnp.where(core == 0, x, y)
    q = jnp.where(core == 0, y, x)
    sp = 1 + 3 * core
    sq = 4 - 3 * core

    def around(value, step):
        return (value + step + 4) % 4

    def at(dp, dq):
        return (rep, lev, (around(p, dp) * sp + around(q, dq) * sq) * 2 + core)

    def at_z(d, where):
        other = (z + d + 8) % 8
        return (other % 2, other // 2, where)

    def near(dz, dt):
        return at_z(dz, (tile + dt + 32) % 32)

    def copy(src, dst, ssem, rsem, where):
        return pltpu.make_async_remote_copy(
            src_ref=src, dst_ref=dst, send_sem=ssem, recv_sem=rsem, device_id=where, device_id_type=MESH
        )

    started = []

    def send(src, dst, ssem, rsem, where):
        c = copy(src, dst, ssem, rsem, where)
        c.start()
        started.append(c)

    def arrived(dst, ssem, rsem):
        copy(dst, dst, ssem, rsem, sib).wait_recv()

    barrier = pltpu.get_barrier_semaphore()
    partners = [sib]
    partners += [at(d, 0) for d in (1, 2, 3)] + [at(0, d) for d in (1, 2, 3)]
    partners += [near(dz, dt) for dz in (1, -1) for dt in (1, -1, 8, -8, 9, -9)]
    partners += [at_z(d, chip * 2 + c) for d in range(1, 8) for c in (0, 1)]
    for partner in partners:
        pl.semaphore_signal(barrier, inc=1, device_id=partner, device_id_type=MESH)

    fetched[0].wait()
    fetched[1].wait()
    for half in range(2):
        for j in range(GROUPS):
            for kind in range(3):
                at_col = kind * D + half * HALF + j * 128
                stage[half, :, j * WIDE + kind * 128:j * WIDE + (kind + 1) * 128] = wq[:, at_col:at_col + 128]
            at_col = half * HALF + j * 128
            stage[half, :, j * WIDE + 384:(j + 1) * WIDE] = wp[:, at_col:at_col + 128]
    for c in fetched[2:]:
        c.wait()
    flag = codes[0, (tile + 31) % 32]
    rows_i = lax.broadcasted_iota(jnp.int32, (TOK, TOK), 0)
    cols_i = lax.broadcasted_iota(jnp.int32, (TOK, TOK), 1)
    order = (cols_i == block_source(rows_i, flag)).astype(F32).astype(BF16)
    blocks[:, :D] = dot(order, tok[...]).astype(BF16)
    blocks[:, D:] = dot(order, upi[...]).astype(BF16)
    leaving = stage[1 - core].astype(F32)
    wout[...] = jnp.concatenate([leaving[:, :D], leaving[:, D:]], axis=0).astype(BF16)
    pl.semaphore_wait(barrier, len(partners))

    send(wout, wsib, w_s, w_r, sib)

    def span(level, group):
        return pl.ds(level * 64 + group * 16, 16)

    for group in range(4):
        for level, dz in ((1, 1), (0, -1)):
            n = (1 - level) * 4 + group
            send(blocks.at[span(level, group)], win.at[span(1 - level, group)], roll_s.at[n], roll_r.at[n],
                 near(dz, -BACK[group]))

    arrived(wsib, w_s, w_r)
    mine = stage[core].astype(F32)
    other = wsib[...].astype(F32)
    other = jnp.concatenate([other[:24], other[24:]], axis=1)
    first = jnp.where(core == 0, mine, other)
    second = jnp.where(core == 0, other, mine)
    chunk = jnp.concatenate([first, second], axis=0).astype(BF16)
    for j in range(GROUPS):
        wbuf[j, q * 4 + p] = chunk[:, j * WIDE:(j + 1) * WIDE]

    def line(buf, j, dq, start=0, count=4):
        return buf.at[j, pl.ds(around(q, dq) * 4 + start, count)]

    def cell(buf, j, dp, dq):
        return buf.at[j, around(q, dq) * 4 + around(p, dp)]

    def gather_first(j):
        own = wbuf.at[j, q * 4 + p]
        for d in (1, 3, 2):
            send(own, own, ga_s.at[j, d], ga_r.at[j, d], at(d, 0))

    def gather_second(j):
        for d in (1, 2, 3):
            arrived(wbuf.at[j, q * 4 + around(p, -d)], ga_s.at[j, d], ga_r.at[j, d])
        send(line(wbuf, j, 0), line(wbuf, j, 0), gb_s.at[j, 0], gb_r.at[j, 0], at(0, 1))
        send(line(wbuf, j, 0), line(wbuf, j, 0), gb_s.at[j, 1], gb_r.at[j, 1], at(0, -1))

    def gather_relay(j):
        arrived(line(wbuf, j, -1), gb_s.at[j, 0], gb_r.at[j, 0])
        send(line(wbuf, j, -1, 0, 3), line(wbuf, j, -1, 0, 3), gb_s.at[j, 2], gb_r.at[j, 2], at(0, 1))
        arrived(line(wbuf, j, 1), gb_s.at[j, 1], gb_r.at[j, 1])
        send(line(wbuf, j, 1, 3, 1), line(wbuf, j, 1, 3, 1), gb_s.at[j, 3], gb_r.at[j, 3], at(0, -1))

    def natural(n):
        return n + core * ((n % 4) * 4 + n // 4 - n)

    def gather_end(j):
        arrived(line(wbuf, j, 2, 0, 3), gb_s.at[j, 2], gb_r.at[j, 2])
        arrived(line(wbuf, j, 2, 3, 1), gb_s.at[j, 3], gb_r.at[j, 3])
        for n in range(16):
            wnat[j, n * CHUNK:(n + 1) * CHUNK, :] = wbuf[j, natural(n)]

    for j in range(GROUPS):
        gather_first(j)
    for j in range(GROUPS):
        gather_second(j)
    gather_relay(0)

    for n in range(8):
        arrived(win.at[pl.ds(n * 16, 16)], roll_s.at[n], roll_r.at[n])
    my_rows = pl.ds(pl.multiple_of(core * TOK, TOK), TOK)
    their_rows = pl.ds(pl.multiple_of((1 - core) * TOK, TOK), TOK)
    ups[my_rows, :] = win[:, D:]
    send(ups.at[my_rows], ups.at[my_rows], sib_s.at[1], sib_r.at[1], sib)
    values = win[:, :D].astype(F32)
    centred = values - jnp.mean(values, axis=1, keepdims=True)
    inverse = lax.rsqrt(jnp.mean(jnp.square(centred), axis=1, keepdims=True) + EPSILON)
    normalized = centred * inverse
    norm[...] = normalized
    inv_ref[...] = jnp.broadcast_to(inverse, (TOK, 128))
    hid[my_rows, :] = normalized.astype(BF16)
    send(hid.at[my_rows], hid.at[my_rows], sib_s.at[0], sib_r.at[0], sib)
    gather_relay(1)
    gather_relay(2)
    arrived(ups.at[their_rows], sib_s.at[1], sib_r.at[1])
    arrived(hid.at[their_rows], sib_s.at[0], sib_r.at[0])
    hid_t[...] = hid[...].T
    ups_t[...] = ups[...].T

    wrapped = jnp.logical_or(z == 0, z == 7)
    allow = jnp.where(wrapped, jnp.where((rows_i >> 6) == (cols_i >> 6), 1.0, 0.0), 1.0).astype(F32)
    allow = jnp.concatenate([allow] * 4, axis=0)
    lane_head = lax.broadcasted_iota(jnp.int32, (TOK, 128), 1) >> 5
    head_masks = [(lane_head == h).astype(F32).astype(BF16) for h in range(4)]

    def stacked(part):
        return jnp.concatenate([part * m for m in head_masks], axis=0)

    def beside(part):
        return jnp.concatenate([part[h * TOK:(h + 1) * TOK] for h in range(4)], axis=1)

    def project(j):
        qkv[...] = dot(hid[...], wnat[j, :, :384]).astype(BF16)
        back[...] = dot(ups[...], wnat[j, :, 384:]).astype(BF16)

    def attend(j):
        for w in range(2):
            rows = slice(w * TOK, (w + 1) * TOK)
            query, key, value = (qkv[rows, kind * 128:(kind + 1) * 128] for kind in range(3))
            coming = back[rows, :]
            query_s, key_s, value_s, coming_s = (stacked(a) for a in (query, key, value, coming))
            raised = jnp.exp(dot_t(query_s, key) * SCALE) * allow
            prob = raised * (1.0 / jnp.sum(raised, axis=1, keepdims=True))
            low = prob.astype(BF16)
            mixed[j, rows, :] = dot(beside(low), value_s).astype(BF16)
            grad_prob = dot_t(coming_s, value)
            centre = jnp.sum(prob * grad_prob, axis=1, keepdims=True)
            grad_scores = (prob * (grad_prob - centre) * SCALE).astype(BF16)
            gtok[j, rows, 0:128] = dot(beside(grad_scores), key_s).astype(BF16)
            gtok[j, rows, 128:256] = t_dot(grad_scores, query_s).astype(BF16)
            gtok[j, rows, 256:384] = t_dot(low, coming_s).astype(BF16)

    def weight_grads(j):
        grad_q = dot(hid_t[...], gtok[j]).astype(BF16)
        grad_p = dot(ups_t[...], mixed[j]).astype(BF16)
        for n in range(16):
            part = slice(n * CHUNK, (n + 1) * CHUNK)
            grad[j, natural(n), :, :384] = grad_q[part]
            grad[j, natural(n), :, 384:] = grad_p[part]

    def outputs_share(j):
        to_output = dot_t(mixed[j], wnat[j, :, 384:])
        to_hidden = dot_t(gtok[j], wnat[j, :, :384])
        if j == 0:
            opart[:, :D] = to_output
            opart[:, D:] = to_hidden
        else:
            opart[:, :D] += to_output
            opart[:, D:] += to_hidden

    def sum_way(j, k, way, dq):
        send(cell(grad, j, ALONG[k], dq), f2.at[j, way, k], f2_s.at[j, way, k], f2_r.at[j, way, k], at(0, dq))

    def sum_start(j):
        for k in range(4):
            if j in DIRECT_OUT:
                for way, dq in ((2, 2), (0, 1), (1, -1)):
                    sum_way(j, k, way, dq)
            else:
                dq = 1 if k in SUM_UP else -1
                send(cell(grad, j, ALONG[k], 2), h2.at[j, k], h2_s.at[j, k], h2_r.at[j, k], at(0, dq))
        if j not in DIRECT_OUT:
            for k in range(4):
                way, dq = (1, -1) if k in SUM_UP else (0, 1)
                sum_way(j, k, way, dq)

    def sum_relay(j):
        if j in DIRECT_OUT:
            return
        for k in range(4):
            way, dq = (0, 1) if k in SUM_UP else (1, -1)
            arrived(h2.at[j, k], h2_s.at[j, k], h2_r.at[j, k])
            place = around(q, dq) * 4 + around(p, ALONG[k])
            grad[j, place] = (grad[j, place].astype(F32) + h2[j, k].astype(F32)).astype(BF16)
            sum_way(j, k, way, dq)

    def sum_first(j):
        for k in range(4):
            total = grad[j, q * 4 + around(p, ALONG[k])].astype(F32)
            for way in (0, 1, 2) if j in DIRECT_OUT else (0, 1):
                arrived(f2.at[j, way, k], f2_s.at[j, way, k], f2_r.at[j, way, k])
                total = total + f2[j, way, k].astype(F32)
            psum[j, k] = total.astype(BF16)
            if k < 3:
                d = (2, 1, 3)[k]
                send(psum.at[j, k], f1.at[j, d], f1_s.at[j, d], f1_r.at[j, d], at(d, 0))

    def sum_z(j):
        total = psum[j, 3].astype(F32)
        for d in (1, 3, 2):
            arrived(f1.at[j, d], f1_s.at[j, d], f1_r.at[j, d])
            total = total + f1[j, d].astype(F32)
        for kind in range(4):
            for r in range(2):
                zs[j, kind * 2 + r] = total[r * 24:(r + 1) * 24, kind * 128:(kind + 1) * 128].astype(BF16)
        for d in (4, 3, 5, 2, 6, 1, 7):
            send(zs.at[j, (z + d) % 8], zr.at[j, d], z1_s.at[j, d], z1_r.at[j, d], at_z(d, chip * 2 + core))

    half_here = z % 2
    slot = (z // 2) * 2 + core
    to_sibling = []

    def hand_out(j):
        total = zs[j, z].astype(F32)
        for d in range(1, 8):
            arrived(zr.at[j, d], z1_s.at[j, d], z1_r.at[j, d])
            total = total + zr[j, d].astype(F32)
        zo[j] = total.astype(BF16)
        for d in (4, 3, 5, 2, 6, 1, 7):
            send(zo.at[j], za.at[j, slot], z2_s.at[j, d], z2_r.at[j, slot], at_z(d, chip * 2 + half_here))
        here = copy(zo.at[j], za.at[j, slot], z2_s.at[j, 0], z2_r.at[j, slot], sib)
        to_sibling.append(here)

        @pl.when(half_here == core)
        def _():
            pltpu.make_async_copy(zo.at[j], za.at[j, slot], own_sem.at[j]).start()

        @pl.when(half_here != core)
        def _():
            here.start()

    def finish(j):
        for n in range(8):
            own = jnp.logical_and(half_here == core, slot == n)

            @pl.when(jnp.logical_not(own))
            def _():
                arrived(za.at[j, n], z2_s.at[j, 0], z2_r.at[j, n])

        @pl.when(half_here == core)
        def _():
            pltpu.make_async_copy(zo.at[j], za.at[j, slot], own_sem.at[j]).wait()

    def give_back():
        arrived(xr, par_s, par_r)
        total = win[:, :D].astype(F32) + opart[my_rows, :D] + xr[:, :D].astype(F32)
        rsend[:, :D] = total.astype(BF16)
        grad_hidden = opart[my_rows, D:] + xr[:, D:].astype(F32)
        normalized = norm[...]
        centre = jnp.mean(grad_hidden, axis=1, keepdims=True)
        along_norm = jnp.mean(grad_hidden * normalized, axis=1, keepdims=True)
        moved = (grad_hidden - centre - normalized * along_norm) * inv_ref[:, :1]
        rsend[:, D:] = (win[:, D:].astype(F32) + moved).astype(BF16)
        for group in range(4):
            for level, dz in ((1, -1), (0, 1)):
                n = level * 4 + group
                send(rsend.at[span(1 - level, group)], rrecv.at[span(level, group)], ret_s.at[n], ret_r.at[n],
                     near(dz, BACK[group]))

    gather_end(0)
    project(0)
    attend(0)
    weight_grads(0)
    sum_start(0)
    gather_end(1)
    project(1)
    attend(1)
    weight_grads(1)
    sum_start(1)
    gather_end(2)
    project(2)
    sum_relay(0)
    attend(2)
    weight_grads(2)
    sum_start(2)
    outputs_share(0)
    sum_relay(1)
    outputs_share(1)
    outputs_share(2)
    xs[...] = opart[their_rows, :].astype(BF16)
    send(xs, xr, par_s, par_r, sib)
    sum_first(0)
    sum_relay(2)
    give_back()
    sum_z(0)
    sum_first(1)
    sum_first(2)
    hand_out(0)
    sum_z(1)
    sum_z(2)

    for n in range(8):
        arrived(rrecv.at[pl.ds(n * 16, 16)], ret_s.at[n], ret_r.at[n])
    order_t = (rows_i == block_source(cols_i, flag)).astype(F32).astype(BF16)
    out_v[...] = dot(order_t, rrecv[:, :D]).astype(BF16)
    gt_v[...] = dot(order_t, rrecv[:, D:]).astype(BF16)
    written = [
        pltpu.make_async_copy(a, b, out_sem.at[i])
        for i, (a, b) in enumerate(((out_v, out_hbm), (gt_v, gt_hbm)))
    ]
    written[0].start()
    written[1].start()
    hand_out(1)
    hand_out(2)
    finish(0)
    finish(1)
    finish(2)
    for c in started:
        c.wait_send()

    @pl.when(half_here != core)
    def _():
        for c in to_sibling:
            c.wait_send()

    for c in written:
        c.wait()


def place_body(out_a, gt_a, za_a, out_b, gt_b, gq_b, gp_b, out_v, gt_v, za_v, gq_v, gp_v, sem):
    reads = [
        pltpu.make_async_copy(a, b, sem.at[0, i]) for i, (a, b) in enumerate(((za_a, za_v), (out_a, out_v), (gt_a, gt_v)))
    ]
    writes = [
        pltpu.make_async_copy(a, b, sem.at[1, i])
        for i, (a, b) in enumerate(((gq_v, gq_b), (gp_v, gp_b), (out_v, out_b), (gt_v, gt_b)))
    ]
    for c in reads:
        c.start()
    reads[0].wait()
    for kind in range(4):
        for j in range(GROUPS):
            for half in range(2):
                piece = za_v[j, kind * 2 + half].astype(F32)
                at_col = half * HALF + j * 128
                if kind < 3:
                    gq_v[:, kind * D + at_col:kind * D + at_col + 128] = piece
                else:
                    gp_v[:, at_col:at_col + 128] = piece
    writes[0].start()
    writes[1].start()
    for k in (1, 2):
        reads[k].wait()
        writes[k + 1].start()
    for c in writes:
        c.wait()


def shards(tokens, w_qkv, w_proj, seam_codes, upstream):
    dma = pltpu.SemaphoreType.DMA
    vmem = pltpu.VMEM
    scratch = [
        vmem((TOK, D), BF16),
        vmem((TOK, D), BF16),
        vmem((24, 3 * D), BF16),
        vmem((24, D), BF16),
        pltpu.SMEM((2, 32), jnp.int32),
        vmem((TOK, 2 * D), BF16),
        vmem((TOK, 2 * D), BF16),
        vmem((2, 24, COLS), BF16),
        vmem((48, D), BF16),
        vmem((48, D), BF16),
        vmem((GROUPS, 16, CHUNK, WIDE), BF16),
        vmem((GROUPS, D, WIDE), BF16),
        vmem((2 * TOK, D), BF16),
        vmem((2 * TOK, D), BF16),
        vmem((D, 2 * TOK), BF16),
        vmem((D, 2 * TOK), BF16),
        vmem((TOK, D), F32),
        vmem((TOK, 128), F32),
        vmem((2 * TOK, 384), BF16),
        vmem((2 * TOK, 128), BF16),
        vmem((GROUPS, 2 * TOK, 128), BF16),
        vmem((GROUPS, 2 * TOK, 384), BF16),
        vmem((2 * TOK, 2 * D), F32),
        vmem((TOK, 2 * D), BF16),
        vmem((TOK, 2 * D), BF16),
        vmem((TOK, 2 * D), BF16),
        vmem((TOK, 2 * D), BF16),
        vmem((GROUPS, 16, CHUNK, WIDE), BF16),
        vmem((GROUPS, 4, CHUNK, WIDE), BF16),
        vmem((GROUPS, 3, 4, CHUNK, WIDE), BF16),
        vmem((GROUPS, 4, CHUNK, WIDE), BF16),
        vmem((GROUPS, 4, CHUNK, WIDE), BF16),
        vmem((GROUPS, 8, 24, 128), BF16),
        vmem((GROUPS, 8, 24, 128), BF16),
        vmem((GROUPS, 24, 128), BF16),
        vmem((TOK, D), BF16),
        vmem((TOK, D), BF16),
        dma((5,)), dma((2,)), dma((GROUPS,)),
        dma((8,)), dma((8,)),
        dma, dma,
        dma((GROUPS, 4)), dma((GROUPS, 4)),
        dma((GROUPS, 4)), dma((GROUPS, 4)),
        dma((2,)), dma((2,)),
        dma, dma,
        dma((8,)), dma((8,)),
        dma((GROUPS, 4)), dma((GROUPS, 4)),
        dma((GROUPS, 3, 4)), dma((GROUPS, 3, 4)),
        dma((GROUPS, 4)), dma((GROUPS, 4)),
        dma((GROUPS, 8)), dma((GROUPS, 8)), dma((GROUPS, 8)), dma((GROUPS, 8)),
    ]
    anywhere = pl.BlockSpec(memory_space=pl.ANY)
    shapes = (
        jax.ShapeDtypeStruct((TOK, D), BF16),
        jax.ShapeDtypeStruct((TOK, D), BF16),
        jax.ShapeDtypeStruct((24, 3 * D), F32),
        jax.ShapeDtypeStruct((24, D), F32),
    )
    pieces = jax.ShapeDtypeStruct((GROUPS, 8, 24, 128), BF16)
    results = pl.pallas_call(
        body,
        out_shape=shapes[:2] + (pieces,),
        in_specs=[anywhere] * 5,
        out_specs=(anywhere,) * 3,
        scratch_shapes=scratch,
        compiler_params=pltpu.CompilerParams(
            collective_id=0, has_side_effects=True, vmem_limit_bytes=56 * 1024 * 1024
        ),
        name="layer",
    )(tokens.reshape(TOK, D), upstream.reshape(TOK, D), w_qkv, w_proj, seam_codes.T)
    out, grad_tok, grad_qkv, grad_proj = pl.pallas_call(
        place_body,
        out_shape=shapes,
        in_specs=[anywhere] * 3,
        out_specs=(anywhere,) * 4,
        scratch_shapes=[vmem(a.shape, a.dtype) for a in shapes[:2] + (pieces,) + shapes[2:]] + [dma((2, 4))],
        name="place",
    )(*results)
    return (out.reshape(tokens.shape), grad_tok.reshape(tokens.shape), grad_qkv, grad_proj)


def solution(mesh):
    field = P("rep", "lev", "tile", None, None, None)
    rows = P("tile", None)
    return jax.shard_map(
        shards,
        mesh=mesh,
        in_specs=(field, rows, rows, P(), field),
        out_specs=(field, field, rows, rows),
        check_vma=False,
    )
```

```python
import functools

import jax
import jax.numpy as jnp
from jax import lax
from jax.experimental import pallas as pl
from jax.experimental.pallas import tpu as pltpu
from jax.sharding import PartitionSpec as P

EPSILON = 1e-05
SCALE = 32 ** (-0.5)
MESH = pl.DeviceIdType.MESH
F32 = jnp.float32
BF16 = jnp.bfloat16
D = 768
HALF = 384
COLS = 4 * HALF
GROUPS = 3
WIDE = COLS // GROUPS
ALONG = (2, 1, -1, 0)
SUM_UP = (0,)
DIRECT_OUT = ()
CHUNK = 48
TOK = 128

BACK = (0, 8, 1, 9)


def dot(a, b):
    return jnp.dot(a, b, preferred_element_type=F32)


def dot_t(a, b):
    return lax.dot_general(a, b, (((1,), (1,)), ((), ())), preferred_element_type=F32)


def t_dot(a, b):
    return lax.dot_general(a, b, (((0,), (0,)), ((), ())), preferred_element_type=F32)


def block_source(block_row, flag):
    group = (block_row >> 4) & 3
    n = block_row & 15
    east = group >> 1
    high = 1 - ((group & 1) ^ (flag * east))
    row = (n >> 2) + 4 * high
    col = (n & 3) + 4 * (1 - east)
    return ((block_row >> 6) << 6) + row * 8 + col


def body(
    tok_hbm, upi_hbm, wq_hbm, wp_hbm, codes_hbm,
    out_hbm, gt_hbm, za,
    tok, upi, wq, wp, codes, blocks, win, stage, wout, wsib, wbuf, wnat, hid, ups, hid_t, ups_t, norm, inv_ref,
    qkv, back, mixed, gtok, opart, xs, xr, rsend, rrecv, grad, h2, f2, psum, f1, zs, zr, zo,
    out_v, gt_v,
    in_sem, out_sem, own_sem,
    roll_s, roll_r, w_s, w_r, ga_s, ga_r, gb_s, gb_r, sib_s, sib_r, par_s, par_r, ret_s, ret_r,
    h2_s, h2_r, f2_s, f2_r, f1_s, f1_r, z1_s, z1_r, z2_s, z2_r,
):
    fetched = [
        pltpu.make_async_copy(a, b, in_sem.at[i])
        for i, (a, b) in enumerate(((wq_hbm, wq), (wp_hbm, wp), (codes_hbm, codes), (tok_hbm, tok), (upi_hbm, upi)))
    ]
    for c in fetched:
        c.start()

    rep = lax.axis_index("rep")
    lev = lax.axis_index("lev")
    tile = lax.axis_index("tile")
    core = tile % 2
    chip = tile // 2
    x = chip % 4
    y = chip // 4
    z = lev * 2 + rep
    sib = (rep, lev, chip * 2 + (1 - core))
    p = jnp.where(core == 0, x, y)
    q = jnp.where(core == 0, y, x)
    sp = 1 + 3 * core
    sq = 4 - 3 * core

    def around(value, step):
        return (value + step + 4) % 4

    def at(dp, dq):
        return (rep, lev, (around(p, dp) * sp + around(q, dq) * sq) * 2 + core)

    def at_z(d, where):
        other = (z + d + 8) % 8
        return (other % 2, other // 2, where)

    def near(dz, dt):
        return at_z(dz, (tile + dt + 32) % 32)

    def copy(src, dst, ssem, rsem, where):
        return pltpu.make_async_remote_copy(
            src_ref=src, dst_ref=dst, send_sem=ssem, recv_sem=rsem, device_id=where, device_id_type=MESH
        )

    started = []

    def send(src, dst, ssem, rsem, where):
        c = copy(src, dst, ssem, rsem, where)
        c.start()
        started.append(c)

    def arrived(dst, ssem, rsem):
        copy(dst, dst, ssem, rsem, sib).wait_recv()

    barrier = pltpu.get_barrier_semaphore()
    partners = [sib]
    partners += [at(d, 0) for d in (1, 2, 3)] + [at(0, d) for d in (1, 2, 3)]
    partners += [near(dz, dt) for dz in (1, -1) for dt in (1, -1, 8, -8, 9, -9)]
    partners += [at_z(d, chip * 2 + c) for d in range(1, 8) for c in (0, 1)]
    for partner in partners:
        pl.semaphore_signal(barrier, inc=1, device_id=partner, device_id_type=MESH)

    fetched[0].wait()
    fetched[1].wait()
    for half in range(2):
        for j in range(GROUPS):
            for kind in range(3):
                at_col = kind * D + half * HALF + j * 128
                stage[half, :, j * WIDE + kind * 128:j * WIDE + (kind + 1) * 128] = wq[:, at_col:at_col + 128]
            at_col = half * HALF + j * 128
            stage[half, :, j * WIDE + 384:(j + 1) * WIDE] = wp[:, at_col:at_col + 128]
    for c in fetched[2:]:
        c.wait()
    flag = codes[0, (tile + 31) % 32]
    rows_i = lax.broadcasted_iota(jnp.int32, (TOK, TOK), 0)
    cols_i = lax.broadcasted_iota(jnp.int32, (TOK, TOK), 1)
    order = (cols_i == block_source(rows_i, flag)).astype(F32).astype(BF16)
    blocks[:, :D] = dot(order, tok[...]).astype(BF16)
    blocks[:, D:] = dot(order, upi[...]).astype(BF16)
    leaving = stage[1 - core].astype(F32)
    wout[...] = jnp.concatenate([leaving[:, :D], leaving[:, D:]], axis=0).astype(BF16)
    pl.semaphore_wait(barrier, len(partners))

    send(wout, wsib, w_s, w_r, sib)

    def span(level, group):
        return pl.ds(level * 64 + group * 16, 16)

    for group in range(4):
        for level, dz in ((1, 1), (0, -1)):
            n = (1 - level) * 4 + group
            send(blocks.at[span(level, group)], win.at[span(1 - level, group)], roll_s.at[n], roll_r.at[n],
                 near(dz, -BACK[group]))

    arrived(wsib, w_s, w_r)
    mine = stage[core].astype(F32)
    other = wsib[...].astype(F32)
    other = jnp.concatenate([other[:24], other[24:]], axis=1)
    first = jnp.where(core == 0, mine, other)
    second = jnp.where(core == 0, other, mine)
    chunk = jnp.concatenate([first, second], axis=0).astype(BF16)
    for j in range(GROUPS):
        wbuf[j, q * 4 + p] = chunk[:, j * WIDE:(j + 1) * WIDE]

    def line(buf, j, dq, start=0, count=4):
        return buf.at[j, pl.ds(around(q, dq) * 4 + start, count)]

    def cell(buf, j, dp, dq):
        return buf.at[j, around(q, dq) * 4 + around(p, dp)]

    def gather_first(j):
        own = wbuf.at[j, q * 4 + p]
        for d in (1, 3, 2):
            send(own, own, ga_s.at[j, d], ga_r.at[j, d], at(d, 0))

    def gather_second(j):
        for d in (1, 2, 3):
            arrived(wbuf.at[j, q * 4 + around(p, -d)], ga_s.at[j, d], ga_r.at[j, d])
        send(line(wbuf, j, 0), line(wbuf, j, 0), gb_s.at[j, 0], gb_r.at[j, 0], at(0, 1))
        send(line(wbuf, j, 0), line(wbuf, j, 0), gb_s.at[j, 1], gb_r.at[j, 1], at(0, -1))

    def gather_relay(j):
        arrived(line(wbuf, j, -1), gb_s.at[j, 0], gb_r.at[j, 0])
        send(line(wbuf, j, -1, 0, 3), line(wbuf, j, -1, 0, 3), gb_s.at[j, 2], gb_r.at[j, 2], at(0, 1))
        arrived(line(wbuf, j, 1), gb_s.at[j, 1], gb_r.at[j, 1])
        send(line(wbuf, j, 1, 3, 1), line(wbuf, j, 1, 3, 1), gb_s.at[j, 3], gb_r.at[j, 3], at(0, -1))

    def natural(n):
        return n + core * ((n % 4) * 4 + n // 4 - n)

    def gather_end(j):
        arrived(line(wbuf, j, 2, 0, 3), gb_s.at[j, 2], gb_r.at[j, 2])
        arrived(line(wbuf, j, 2, 3, 1), gb_s.at[j, 3], gb_r.at[j, 3])
        for n in range(16):
            wnat[j, n * CHUNK:(n + 1) * CHUNK, :] = wbuf[j, natural(n)]

    for j in range(GROUPS):
        gather_first(j)
    for j in range(GROUPS):
        gather_second(j)
    gather_relay(0)

    for n in range(8):
        arrived(win.at[pl.ds(n * 16, 16)], roll_s.at[n], roll_r.at[n])
    my_rows = pl.ds(pl.multiple_of(core * TOK, TOK), TOK)
    their_rows = pl.ds(pl.multiple_of((1 - core) * TOK, TOK), TOK)
    ups[my_rows, :] = win[:, D:]
    send(ups.at[my_rows], ups.at[my_rows], sib_s.at[1], sib_r.at[1], sib)
    values = win[:, :D].astype(F32)
    centred = values - jnp.mean(values, axis=1, keepdims=True)
    inverse = lax.rsqrt(jnp.mean(jnp.square(centred), axis=1, keepdims=True) + EPSILON)
    normalized = centred * inverse
    norm[...] = normalized
    inv_ref[...] = jnp.broadcast_to(inverse, (TOK, 128))
    hid[my_rows, :] = normalized.astype(BF16)
    send(hid.at[my_rows], hid.at[my_rows], sib_s.at[0], sib_r.at[0], sib)
    gather_relay(1)
    gather_relay(2)
    arrived(ups.at[their_rows], sib_s.at[1], sib_r.at[1])
    arrived(hid.at[their_rows], sib_s.at[0], sib_r.at[0])

    wrapped = jnp.logical_or(z == 0, z == 7)
    allow = jnp.where(wrapped, jnp.where((rows_i >> 6) == (cols_i >> 6), 1.0, 0.0), 1.0).astype(F32)
    allow = jnp.concatenate([allow] * 4, axis=0)
    lane_head = lax.broadcasted_iota(jnp.int32, (TOK, 128), 1) >> 5
    head_masks = [(lane_head == h).astype(F32).astype(BF16) for h in range(4)]

    def stacked(part):
        return jnp.concatenate([part * m for m in head_masks], axis=0)

    def beside(part):
        return jnp.concatenate([part[h * TOK:(h + 1) * TOK] for h in range(4)], axis=1)

    def project(j):
        qkv[...] = dot(hid[...], wnat[j, :, :384]).astype(BF16)
        back[...] = dot(ups[...], wnat[j, :, 384:]).astype(BF16)

    def attend(j):
        for w in range(2):
            rows = slice(w * TOK, (w + 1) * TOK)
            query, key, value = (qkv[rows, kind * 128:(kind + 1) * 128] for kind in range(3))
            coming = back[rows, :]
            query_s, key_s, value_s, coming_s = (stacked(a) for a in (query, key, value, coming))
            raised = jnp.exp(dot_t(query_s, key) * SCALE) * allow
            prob = raised * (1.0 / jnp.sum(raised, axis=1, keepdims=True))
            low = prob.astype(BF16)
            mixed[j, rows, :] = dot(beside(low), value_s).astype(BF16)
            grad_prob = dot_t(coming_s, value)
            centre = jnp.sum(prob * grad_prob, axis=1, keepdims=True)
            grad_scores = (prob * (grad_prob - centre) * SCALE).astype(BF16)
            gtok[j, rows, 0:128] = dot(beside(grad_scores), key_s).astype(BF16)
            gtok[j, rows, 128:256] = t_dot(grad_scores, query_s).astype(BF16)
            gtok[j, rows, 256:384] = t_dot(low, coming_s).astype(BF16)

    def weight_grads(j):
        grad_q = dot(hid_t[...], gtok[j]).astype(BF16)
        grad_p = dot(ups_t[...], mixed[j]).astype(BF16)
        for n in range(16):
            part = slice(n * CHUNK, (n + 1) * CHUNK)
            grad[j, natural(n), :, :384] = grad_q[part]
            grad[j, natural(n), :, 384:] = grad_p[part]

    def outputs_share(j):
        to_output = dot_t(mixed[j], wnat[j, :, 384:])
        to_hidden = dot_t(gtok[j], wnat[j, :, :384])
        if j == 0:
            opart[:, :D] = to_output
            opart[:, D:] = to_hidden
        else:
            opart[:, :D] += to_output
            opart[:, D:] += to_hidden

    def sum_way(j, k, way, dq):
        send(cell(grad, j, ALONG[k], dq), f2.at[j, way, k], f2_s.at[j, way, k], f2_r.at[j, way, k], at(0, dq))

    def sum_start(j):
        for k in range(4):
            if j in DIRECT_OUT:
                for way, dq in ((2, 2), (0, 1), (1, -1)):
                    sum_way(j, k, way, dq)
            else:
                dq = 1 if k in SUM_UP else -1
                send(cell(grad, j, ALONG[k], 2), h2.at[j, k], h2_s.at[j, k], h2_r.at[j, k], at(0, dq))
        if j not in DIRECT_OUT:
            for k in range(4):
                way, dq = (1, -1) if k in SUM_UP else (0, 1)
                sum_way(j, k, way, dq)

    def sum_relay(j):
        if j in DIRECT_OUT:
            return
        for k in range(4):
            way, dq = (0, 1) if k in SUM_UP else (1, -1)
            arrived(h2.at[j, k], h2_s.at[j, k], h2_r.at[j, k])
            place = around(q, dq) * 4 + around(p, ALONG[k])
            grad[j, place] = (grad[j, place].astype(F32) + h2[j, k].astype(F32)).astype(BF16)
            sum_way(j, k, way, dq)

    def sum_first(j):
        for k in range(4):
            total = grad[j, q * 4 + around(p, ALONG[k])].astype(F32)
            for way in (0, 1, 2) if j in DIRECT_OUT else (0, 1):
                arrived(f2.at[j, way, k], f2_s.at[j, way, k], f2_r.at[j, way, k])
                total = total + f2[j, way, k].astype(F32)
            psum[j, k] = total.astype(BF16)
            if k < 3:
                d = (2, 1, 3)[k]
                send(psum.at[j, k], f1.at[j, d], f1_s.at[j, d], f1_r.at[j, d], at(d, 0))

    def sum_z(j):
        total = psum[j, 3].astype(F32)
        for d in (1, 3, 2):
            arrived(f1.at[j, d], f1_s.at[j, d], f1_r.at[j, d])
            total = total + f1[j, d].astype(F32)
        for kind in range(4):
            for r in range(2):
                zs[j, kind * 2 + r] = total[r * 24:(r + 1) * 24, kind * 128:(kind + 1) * 128].astype(BF16)
        for d in (4, 3, 5, 2, 6, 1, 7):
            send(zs.at[j, (z + d) % 8], zr.at[j, d], z1_s.at[j, d], z1_r.at[j, d], at_z(d, chip * 2 + core))

    half_here = z % 2
    slot = (z // 2) * 2 + core
    to_sibling = []

    def hand_out(j):
        total = zs[j, z].astype(F32)
        for d in range(1, 8):
            arrived(zr.at[j, d], z1_s.at[j, d], z1_r.at[j, d])
            total = total + zr[j, d].astype(F32)
        zo[j] = total.astype(BF16)
        for d in (4, 3, 5, 2, 6, 1, 7):
            send(zo.at[j], za.at[j, slot], z2_s.at[j, d], z2_r.at[j, slot], at_z(d, chip * 2 + half_here))
        here = copy(zo.at[j], za.at[j, slot], z2_s.at[j, 0], z2_r.at[j, slot], sib)
        to_sibling.append(here)

        @pl.when(half_here == core)
        def _():
            pltpu.make_async_copy(zo.at[j], za.at[j, slot], own_sem.at[j]).start()

        @pl.when(half_here != core)
        def _():
            here.start()

    def finish(j):
        for n in range(8):
            own = jnp.logical_and(half_here == core, slot == n)

            @pl.when(jnp.logical_not(own))
            def _():
                arrived(za.at[j, n], z2_s.at[j, 0], z2_r.at[j, n])

        @pl.when(half_here == core)
        def _():
            pltpu.make_async_copy(zo.at[j], za.at[j, slot], own_sem.at[j]).wait()

    def give_back():
        arrived(xr, par_s, par_r)
        total = win[:, :D].astype(F32) + opart[my_rows, :D] + xr[:, :D].astype(F32)
        rsend[:, :D] = total.astype(BF16)
        grad_hidden = opart[my_rows, D:] + xr[:, D:].astype(F32)
        normalized = norm[...]
        centre = jnp.mean(grad_hidden, axis=1, keepdims=True)
        along_norm = jnp.mean(grad_hidden * normalized, axis=1, keepdims=True)
        moved = (grad_hidden - centre - normalized * along_norm) * inv_ref[:, :1]
        rsend[:, D:] = (win[:, D:].astype(F32) + moved).astype(BF16)
        for group in range(4):
            for level, dz in ((1, -1), (0, 1)):
                n = level * 4 + group
                send(rsend.at[span(1 - level, group)], rrecv.at[span(level, group)], ret_s.at[n], ret_r.at[n],
                     near(dz, BACK[group]))

    gather_end(0)
    project(0)
    hid_t[...] = hid[...].T
    ups_t[...] = ups[...].T
    attend(0)
    weight_grads(0)
    sum_start(0)
    gather_end(1)
    project(1)
    attend(1)
    weight_grads(1)
    sum_start(1)
    gather_end(2)
    project(2)
    sum_relay(0)
    attend(2)
    weight_grads(2)
    sum_start(2)
    outputs_share(0)
    sum_relay(1)
    outputs_share(1)
    outputs_share(2)
    xs[...] = opart[their_rows, :].astype(BF16)
    send(xs, xr, par_s, par_r, sib)
    sum_first(0)
    sum_relay(2)
    give_back()
    sum_z(0)
    sum_first(1)
    sum_first(2)
    hand_out(0)
    sum_z(1)
    sum_z(2)

    for n in range(8):
        arrived(rrecv.at[pl.ds(n * 16, 16)], ret_s.at[n], ret_r.at[n])
    order_t = (rows_i == block_source(cols_i, flag)).astype(F32).astype(BF16)
    out_v[...] = dot(order_t, rrecv[:, :D]).astype(BF16)
    gt_v[...] = dot(order_t, rrecv[:, D:]).astype(BF16)
    written = [
        pltpu.make_async_copy(a, b, out_sem.at[i])
        for i, (a, b) in enumerate(((out_v, out_hbm), (gt_v, gt_hbm)))
    ]
    written[0].start()
    written[1].start()
    hand_out(1)
    hand_out(2)
    finish(0)
    finish(1)
    finish(2)
    for c in started:
        c.wait_send()

    @pl.when(half_here != core)
    def _():
        for c in to_sibling:
            c.wait_send()

    for c in written:
        c.wait()


def place_body(out_a, gt_a, za_a, out_b, gt_b, gq_b, gp_b, out_v, gt_v, za_v, gq_v, gp_v, sem):
    reads = [
        pltpu.make_async_copy(a, b, sem.at[0, i]) for i, (a, b) in enumerate(((za_a, za_v), (out_a, out_v), (gt_a, gt_v)))
    ]
    writes = [
        pltpu.make_async_copy(a, b, sem.at[1, i])
        for i, (a, b) in enumerate(((gq_v, gq_b), (gp_v, gp_b), (out_v, out_b), (gt_v, gt_b)))
    ]
    for c in reads:
        c.start()
    reads[0].wait()
    for kind in range(4):
        for j in range(GROUPS):
            for half in range(2):
                piece = za_v[j, kind * 2 + half].astype(F32)
                at_col = half * HALF + j * 128
                if kind < 3:
                    gq_v[:, kind * D + at_col:kind * D + at_col + 128] = piece
                else:
                    gp_v[:, at_col:at_col + 128] = piece
    writes[0].start()
    writes[1].start()
    for k in (1, 2):
        reads[k].wait()
        writes[k + 1].start()
    for c in writes:
        c.wait()


def shards(tokens, w_qkv, w_proj, seam_codes, upstream):
    dma = pltpu.SemaphoreType.DMA
    vmem = pltpu.VMEM
    scratch = [
        vmem((TOK, D), BF16),
        vmem((TOK, D), BF16),
        vmem((24, 3 * D), BF16),
        vmem((24, D), BF16),
        pltpu.SMEM((2, 32), jnp.int32),
        vmem((TOK, 2 * D), BF16),
        vmem((TOK, 2 * D), BF16),
        vmem((2, 24, COLS), BF16),
        vmem((48, D), BF16),
        vmem((48, D), BF16),
        vmem((GROUPS, 16, CHUNK, WIDE), BF16),
        vmem((GROUPS, D, WIDE), BF16),
        vmem((2 * TOK, D), BF16),
        vmem((2 * TOK, D), BF16),
        vmem((D, 2 * TOK), BF16),
        vmem((D, 2 * TOK), BF16),
        vmem((TOK, D), F32),
        vmem((TOK, 128), F32),
        vmem((2 * TOK, 384), BF16),
        vmem((2 * TOK, 128), BF16),
        vmem((GROUPS, 2 * TOK, 128), BF16),
        vmem((GROUPS, 2 * TOK, 384), BF16),
        vmem((2 * TOK, 2 * D), F32),
        vmem((TOK, 2 * D), BF16),
        vmem((TOK, 2 * D), BF16),
        vmem((TOK, 2 * D), BF16),
        vmem((TOK, 2 * D), BF16),
        vmem((GROUPS, 16, CHUNK, WIDE), BF16),
        vmem((GROUPS, 4, CHUNK, WIDE), BF16),
        vmem((GROUPS, 3, 4, CHUNK, WIDE), BF16),
        vmem((GROUPS, 4, CHUNK, WIDE), BF16),
        vmem((GROUPS, 4, CHUNK, WIDE), BF16),
        vmem((GROUPS, 8, 24, 128), BF16),
        vmem((GROUPS, 8, 24, 128), BF16),
        vmem((GROUPS, 24, 128), BF16),
        vmem((TOK, D), BF16),
        vmem((TOK, D), BF16),
        dma((5,)), dma((2,)), dma((GROUPS,)),
        dma((8,)), dma((8,)),
        dma, dma,
        dma((GROUPS, 4)), dma((GROUPS, 4)),
        dma((GROUPS, 4)), dma((GROUPS, 4)),
        dma((2,)), dma((2,)),
        dma, dma,
        dma((8,)), dma((8,)),
        dma((GROUPS, 4)), dma((GROUPS, 4)),
        dma((GROUPS, 3, 4)), dma((GROUPS, 3, 4)),
        dma((GROUPS, 4)), dma((GROUPS, 4)),
        dma((GROUPS, 8)), dma((GROUPS, 8)), dma((GROUPS, 8)), dma((GROUPS, 8)),
    ]
    anywhere = pl.BlockSpec(memory_space=pl.ANY)
    shapes = (
        jax.ShapeDtypeStruct((TOK, D), BF16),
        jax.ShapeDtypeStruct((TOK, D), BF16),
        jax.ShapeDtypeStruct((24, 3 * D), F32),
        jax.ShapeDtypeStruct((24, D), F32),
    )
    pieces = jax.ShapeDtypeStruct((GROUPS, 8, 24, 128), BF16)
    results = pl.pallas_call(
        body,
        out_shape=shapes[:2] + (pieces,),
        in_specs=[anywhere] * 5,
        out_specs=(anywhere,) * 3,
        scratch_shapes=scratch,
        compiler_params=pltpu.CompilerParams(
            collective_id=0, has_side_effects=True, vmem_limit_bytes=56 * 1024 * 1024
        ),
        name="layer",
    )(tokens.reshape(TOK, D), upstream.reshape(TOK, D), w_qkv, w_proj, seam_codes.T)
    out, grad_tok, grad_qkv, grad_proj = pl.pallas_call(
        place_body,
        out_shape=shapes,
        in_specs=[anywhere] * 3,
        out_specs=(anywhere,) * 4,
        scratch_shapes=[vmem(a.shape, a.dtype) for a in shapes[:2] + (pieces,) + shapes[2:]] + [dma((2, 4))],
        name="place",
    )(*results)
    return (out.reshape(tokens.shape), grad_tok.reshape(tokens.shape), grad_qkv, grad_proj)


def solution(mesh):
    field = P("rep", "lev", "tile", None, None, None)
    rows = P("tile", None)
    return jax.shard_map(
        shards,
        mesh=mesh,
        in_specs=(field, rows, rows, P(), field),
        out_specs=(field, field, rows, rows),
        check_vma=False,
    )
```
